32 devices in a mesh: sect: 4 (over x, core), batch: 8 (over z, y).
Axes of the slice: x: 2, y: 2, z: 4, core: 2. Of those that a mesh axis runs over, the one named last changes fastest.
Arguments:
- warm: bfloat16 [8192, 640], P(('sect', 'batch')), may hold values from -6 to 6
- latents: float32 [4, 1024], P(None, 'batch'), may hold values from -6 to 6
- timesteps: int32 [5], replicated, may hold values from 300 to 599
- assign: int32 [8], P('batch'), may hold values from 0 to 7, each once
- prompts: bfloat16 [8, 640], P('batch'), may hold values from -6 to 6
- w_in: bfloat16 [2560, 2560], P('sect'), may hold values from -0.25 to 0.25
- time_w: bfloat16 [2560, 640], P('sect'), may hold values from -0.25 to 0.25
- w_out: bfloat16 [5120, 640], P(('sect', 'batch')), may hold values from -0.15625 to 0.15625
- conv_in_w: bfloat16 [4, 640], replicated, may hold values from -3 to 3
- conv_out_w: bfloat16 [4, 640], replicated, may hold values from -0.25 to 0.25
Outputs:
- segments: bfloat16 [8192, 640], P(('sect', 'batch'))
- final_latents: float32 [4, 1024], P('sect', 'batch')
The draws below stay inside these ranges and needn't reach their ends.
Inputs may be any that keep to these rules, and one draw needn't show every extreme that they name: `assign`: each prompt is assigned to exactly one prompt batch.
All inputs are finite; a program needn't handle non-finite values.
Results may differ from the reference program's by a relative error of at most 0.015.
Values may be sent and summed in bfloat16 or wider, within the bound.
A program may use at most 64 MiB of HBM per device.

```python
import math
import jax
import jax.numpy as jnp
from jax import lax

C = 640
FFI = 1280
LAT = 4
P_SIZE = 128
STEPS = 4
PROMPTS = 8
LAT_COLS = 1024
SEGMENT_ROWS = 8192
N_SECT = 4
N_BATCH = 8


def with_ends(entries, key, least, top_value):
    longest = entries.shape.index(max(entries.shape))
    spots = []
    for shift in (0, 1):
        where = [jax.random.randint(jax.random.fold_in(key, axis), (), 0, length) for axis, length in enumerate(entries.shape)]
        where[longest] = (where[longest] + shift) % entries.shape[longest]
        spots.append(tuple(where))
    return entries.at[spots[0]].set(least).at[spots[1]].set(top_value)


def level_of(own_key, dims, pieces, smallest, top_value):
    loudness, own = 1.0, jax.random.fold_in(own_key, 6)
    for dim, blocks in pieces:
        heights = jnp.exp(jax.random.uniform(jax.random.fold_in(own, dim), (blocks,), jnp.float32, smallest / len(pieces), top_value / len(pieces)))
        loudness = loudness * jnp.repeat(heights, dims[dim] // blocks).reshape([-1 if axis == dim else 1 for axis in range(len(dims))])
    return loudness


def bell_draw(key, extent, deviation, most, shards=(), held_as=jnp.bfloat16):
    level = level_of(key, extent, shards, -0.22, 0.18) if shards else 1.0
    result = jax.random.normal(key, extent, jnp.float32) * deviation * level
    return jnp.minimum(jnp.maximum(result, -most), most).astype(held_as)


def setup_inputs(seed: int = 0) -> dict:
    splits = jax.random.split(jax.random.key(seed), 11)
    warm = bell_draw(splits[0], (SEGMENT_ROWS, C), 1.0, 6.0, ((0, 32),))
    latents = bell_draw(splits[1], (LAT, LAT_COLS), 1.0, 6.0, ((1, 8),), jnp.float32)
    timesteps = with_ends(jax.random.randint(splits[2], (STEPS + 1,), 300, 600), jax.random.fold_in(splits[2], 1), 300, 599).astype(jnp.int32)
    assign = jax.random.permutation(splits[3], PROMPTS).astype(jnp.int32)
    prompts = bell_draw(splits[4], (PROMPTS, C), 1.0, 6.0, ((0, 8),))
    w_in = bell_draw(splits[5], (N_SECT * C, 2 * FFI), C ** -0.5, 0.25, ((0, 4),))
    time_w = bell_draw(splits[6], (N_SECT * C, C), C ** -0.5, 0.25, ((0, 4),))
    w_out = bell_draw(splits[7], (N_SECT * FFI, C), FFI ** -0.5, 0.15625, ((0, 32),))
    conv_in_w = bell_draw(splits[8], (LAT, C), LAT ** -0.5, 3.0)
    conv_out_w = bell_draw(splits[9], (LAT, C), C ** -0.5, 0.25)
    return {"warm": warm, "latents": latents, "timesteps": timesteps, "assign": assign, "prompts": prompts, "w_in": w_in, "time_w": time_w, "w_out": w_out, "conv_in_w": conv_in_w, "conv_out_w": conv_out_w}


guidance_scale = 3.0

def sinusoid(time_value, channels):
    half_width = channels // 2
    frequency = jnp.exp(-math.log(10000.0) * jnp.arange(half_width, dtype=jnp.float32) / half_width)
    angles = time_value.astype(jnp.float32) * frequency
    return jnp.concatenate([jnp.cos(angles), jnp.sin(angles)])

def alpha_bar(time_value):
    phase_angle = (time_value.astype(jnp.float32) / 1000.0 + 0.008) / 1.008 * (math.pi / 2)
    return jnp.cos(phase_angle) ** 2

def rms_norm(values):
    return values * lax.rsqrt(lax.optimization_barrier(jnp.mean(values * values, axis=-1, keepdims=True)) + 1e-06)

def feed_block(inputs, time_vec, cond_rows, weight_in, weight_out, hidden_units):
    summed = inputs + time_vec + cond_rows
    normed = rms_norm(summed).astype(jnp.bfloat16)
    projected = jnp.dot(normed, weight_in, preferred_element_type=jnp.float32)
    hidden = (projected[:, :hidden_units] * jax.nn.gelu(projected[:, hidden_units:], approximate=False)).astype(jnp.bfloat16)
    return (summed + jnp.dot(hidden, weight_out, preferred_element_type=jnp.float32)).astype(jnp.bfloat16)

def reference(warm, latents, timesteps, assign, prompts, w_in, time_w, w_out, conv_in_w, conv_out_w):
    rows = 2 * P_SIZE
    whole = N_BATCH * rows
    segment_list = [warm[section * whole:(section + 1) * whole] for section in range(N_SECT)]
    chosen = prompts[assign].astype(jnp.float32)
    cond = jnp.concatenate([jnp.broadcast_to(chosen[:, None, :], (N_BATCH, P_SIZE, C)), jnp.zeros((N_BATCH, P_SIZE, C), jnp.float32)], axis=1).reshape(whole, C)
    latent = latents
    for step_index in range(STEPS):
        time_now = timesteps[step_index]
        time_next = timesteps[step_index + 1]
        embedded = jax.nn.silu(sinusoid(time_now, C)).astype(jnp.bfloat16)
        latent_bf = latent.astype(jnp.bfloat16).astype(jnp.float32).reshape(LAT, N_BATCH, P_SIZE)
        first = jnp.einsum('lbp,lc->bpc', latent_bf, conv_in_w.astype(jnp.float32)).astype(jnp.bfloat16)
        first = jnp.concatenate([first, first], axis=1).reshape(whole, C)
        new_list = []
        for section in range(N_SECT):
            if section == 0:
                inputs = first.astype(jnp.float32)
            else:
                inputs = segment_list[section - 1].astype(jnp.float32)
            skip_rows = segment_list[(section + 1) % N_SECT].astype(jnp.float32)
            inputs = (inputs + skip_rows) * 0.5
            time_vec = jnp.dot(embedded[None, :], time_w[section * C:(section + 1) * C], preferred_element_type=jnp.float32)
            new_list.append(feed_block(inputs, time_vec, cond, w_in[section * C:(section + 1) * C], w_out[section * FFI:(section + 1) * FFI], FFI))
        final_segment = new_list[-1]
        activated = jax.nn.silu(rms_norm(final_segment.astype(jnp.float32))).astype(jnp.bfloat16)
        noise = jnp.einsum('lc,bqc->lbq', conv_out_w.astype(jnp.float32), activated.astype(jnp.float32).reshape(N_BATCH, rows, C))
        guided = noise[:, :, P_SIZE:] + guidance_scale * (noise[:, :, :P_SIZE] - noise[:, :, P_SIZE:])
        guided = guided.reshape(LAT, N_BATCH * P_SIZE)
        bar_now = alpha_bar(time_now)
        bar_next = alpha_bar(time_next)
        clean = (latent - jnp.sqrt(1.0 - bar_now) * guided) / jnp.sqrt(bar_now)
        latent = jnp.sqrt(bar_next) * clean + jnp.sqrt(1.0 - bar_next) * guided
        segment_list = new_list
    return (jnp.concatenate(segment_list, axis=0), latent)
```

```python
import functools
import math

import jax
import jax.numpy as jnp
from jax import lax
from jax.experimental import pallas as pl
from jax.experimental.pallas import tpu as pltpu
from jax.sharding import PartitionSpec as P

guidance_scale = 3.0
MESH = pl.DeviceIdType.MESH
F32 = jnp.float32
BF16 = jnp.bfloat16
CHUNKS = 2
SPLIT = (128, 128, 128, 128, 128)
DETOUR = (1, 3)
LEAD = 1


def column_pieces(channels):
    widths = SPLIT if sum(SPLIT) == channels else (channels,)
    return [(sum(widths[:j]), width) for j, width in enumerate(widths)]


def kernel(
    sects, batches, gathered,
    ts_hbm, assign_hbm, warm_ref, lat_hbm, prompts_hbm, w_in_ref, time_w_ref, w_out_ref, cin_hbm, cout_hbm,
    oseg_ref, olat_ref,
    ts_ref, assign_ref, lat_ref, prompts_ref, cin_ref, cout_ref,
    w_in, time_w, w_all, xbuf, kbuf, ybuf, a_scr, h_scr, tv, roots, rests, cond, ptab,
    cin, cout, lat, latin, latout, fin, fin_in,
    ready, turn, load_sem, x_send, x_recv, k_send, k_recv, l_send, l_recv, f_send, f_recv,
    p_send, p_recv, g_line, g_side, g_recv, xc_send, xc_recv, kc_send, kc_recv,
):
    s = lax.axis_index("sect")
    me = lax.axis_index("batch")
    steps = ts_ref.shape[0] - 1
    _, positions, channels = warm_ref.shape
    hidden = w_all.shape[0]
    part = positions // CHUNKS
    up = lax.rem(s + 1, sects)
    down = lax.rem(s + sects - 1, sects)
    last = sects - 1
    pieces = column_pieces(channels)
    final_piece = len(pieces) - 1

    loads = [
        pltpu.make_async_copy(time_w_ref, time_w, load_sem.at[0]),
        pltpu.make_async_copy(w_in_ref, w_in, load_sem.at[1]),
    ]
    if gathered:
        loads.append(pltpu.make_async_copy(w_out_ref, w_all, load_sem.at[2]))
    else:
        depth = w_out_ref.shape[0]
        own_rows = pl.ds(pl.multiple_of(me * depth, depth), depth)
        loads.append(pltpu.make_async_copy(w_out_ref, w_all.at[own_rows], load_sem.at[2]))
    pairs = [(prompts_hbm, prompts_ref), (ts_hbm, ts_ref), (assign_hbm, assign_ref), (lat_hbm, lat_ref),
             (cin_hbm, cin_ref), (cout_hbm, cout_ref)]
    for j, (src, dst) in enumerate(pairs):
        loads.append(pltpu.make_async_copy(src, dst, load_sem.at[3 + j]))
    for copy in loads[3:] + loads[:3]:
        copy.start()

    barrier = pltpu.get_barrier_semaphore()
    for d in range(1, sects):
        pl.semaphore_signal(barrier, inc=1, device_id={"sect": lax.rem(s + d, sects)}, device_id_type=MESH)
    met = sects - 1
    if not gathered:
        z, y = me // 2, lax.rem(me, 2)
        length = batches // 2
        side = z * 2 + (1 - y)
        pl.semaphore_signal(barrier, inc=1, device_id={"batch": side}, device_id_type=MESH)
        for d in range(1, length):
            @pl.when(z + d < length)
            def _(d=d):
                for b in (me + 2 * d, side + 2 * d):
                    pl.semaphore_signal(barrier, inc=1, device_id={"batch": b}, device_id_type=MESH)
        met = met + 1 + 2 * z
        loads[3].wait()
        ptab[me] = prompts_ref[...].astype(F32)
    pl.semaphore_wait(barrier, met)
    if not gathered:
        for d in range(1, length):
            @pl.when(z >= d)
            def _(d=d):
                for b in (me - 2 * d, side - 2 * d):
                    pl.semaphore_signal(ready.at[2], inc=1, device_id={"batch": b}, device_id_type=MESH)
                if d < 3:
                    pl.semaphore_signal(ready.at[d - 1], inc=1, device_id={"batch": me - 2 * d}, device_id_type=MESH)

    def rows(c):
        return pl.ds(c * part, part)

    def x_copy(src, slot, c):
        return pltpu.make_async_remote_copy(
            src_ref=src, dst_ref=xbuf.at[slot, :, rows(c), :], send_sem=x_send.at[slot, c],
            recv_sem=x_recv.at[slot, c], device_id={"sect": up}, device_id_type=MESH)

    def k_copy(src, slot, c):
        return pltpu.make_async_remote_copy(
            src_ref=src, dst_ref=kbuf.at[slot, :, rows(c), :], send_sem=k_send.at[slot, c],
            recv_sem=k_recv.at[slot, c], device_id={"sect": down}, device_id_type=MESH)

    def columns(ref, j, c=None):
        at, width = pieces[j]
        return ref.at[1, :, slice(None) if c is None else rows(c), pl.ds(at, width)]

    def x_part(j, c=None):
        sems = (xc_send.at[j], xc_recv.at[j]) if c is None else (x_send.at[1, c], x_recv.at[1, c])
        return pltpu.make_async_remote_copy(
            src_ref=columns(ybuf, j, c), dst_ref=columns(xbuf, j, c), send_sem=sems[0],
            recv_sem=sems[1], device_id={"sect": up}, device_id_type=MESH)

    def k_part(j, c=None):
        sems = (kc_send.at[j], kc_recv.at[j]) if c is None else (k_send.at[1, c], k_recv.at[1, c])
        return pltpu.make_async_remote_copy(
            src_ref=columns(ybuf, j, c), dst_ref=columns(kbuf, j, c), send_sem=sems[0],
            recv_sem=sems[1], device_id={"sect": down}, device_id_type=MESH)

    def l_copy(slot, c):
        return pltpu.make_async_remote_copy(
            src_ref=latout.at[slot, rows(c), :], dst_ref=latin.at[slot, rows(c), :], send_sem=l_send.at[slot, c],
            recv_sem=l_recv.at[slot, c], device_id={"sect": 0}, device_id_type=MESH)

    def f_copy(d):
        return pltpu.make_async_remote_copy(
            src_ref=fin.at[d], dst_ref=fin_in, send_sem=f_send.at[d],
            recv_sem=f_recv, device_id={"sect": d}, device_id_type=MESH)

    if not gathered:
        def p_copy(b):
            return pltpu.make_async_remote_copy(
                src_ref=ptab.at[me], dst_ref=ptab.at[me], send_sem=p_send.at[b], recv_sem=p_recv.at[me],
                device_id={"batch": b}, device_id_type=MESH)

        def p_down(act):
            act(p_copy(side))
            for d in range(1, length):
                @pl.when(z >= d)
                def _(d=d):
                    act(p_copy(me - 2 * d))
                    act(p_copy(side - 2 * d))

        def p_up(act):
            for d in range(1, length):
                @pl.when(z + d < length)
                def _(d=d):
                    act(p_copy(me + 2 * d))
                    act(p_copy(side + 2 * d))

        def block(j, b):
            at, width = pieces[j]
            return w_all.at[pl.ds(pl.multiple_of(b * depth, depth), depth), pl.ds(at, width)]

        def g_copy(j, b, to, sem, own):
            at, width = pieces[j]
            return pltpu.make_async_remote_copy(
                src_ref=w_out_ref.at[:, pl.ds(at, width)] if own else block(j, b), dst_ref=block(j, b), send_sem=sem,
                recv_sem=g_recv.at[j, b], device_id={"batch": to}, device_id_type=MESH)

        def g_line_copy(j, b, d, own=False):
            return g_copy(j, b, me + 2 * d, g_line.at[2 * abs(d) - (2 if d > 0 else 1), j, b], own)

        def g_side_copy(j, b, own=False):
            return g_copy(j, b, side, g_side.at[j, b], own)

        def g_arrived(j, b):
            pltpu.make_async_copy(block(j, b), block(j, b), g_recv.at[j, b]).wait()

        def own_low(j, act):
            @pl.when(z >= 1)
            def _():
                act(g_line_copy(j, me, -1, True))
            act(g_side_copy(j, me, True))

            @pl.when(z >= 2)
            def _():
                act(g_line_copy(j, me, -2, True))

        def own_up(j, d, act):
            @pl.when(z + d < length)
            def _():
                act(g_line_copy(j, me, d, True))

        def near(j, act, arrive):
            detour = j in DETOUR

            @pl.when(z + 1 < length)
            def _():
                b = me + 2
                if arrive:
                    g_arrived(j, b)
                if detour:
                    @pl.when(z > 0)
                    def _():
                        act(g_side_copy(j, b))
                else:
                    act(g_side_copy(j, b))

            @pl.when(z >= 1)
            def _():
                b = me - 2
                if arrive:
                    g_arrived(j, b)
                if not detour:
                    act(g_side_copy(j, b))

        def middle(j, act, arrive):
            @pl.when(z + 2 < length)
            def _():
                b = me + 4
                if arrive:
                    g_arrived(j, b)

                @pl.when(z > 0)
                def _():
                    act(g_line_copy(j, b, -1))
                act(g_side_copy(j, b))

            @pl.when(z >= 2)
            def _():
                b = me - 4
                if arrive:
                    g_arrived(j, b)

                @pl.when(z + 1 < length)
                def _():
                    act(g_line_copy(j, b, 1))
                act(g_side_copy(j, b))

        def far(j, act, arrive):
            for d in (3, -3):
                @pl.when((z + d < length) & (z + d >= 0))
                def _(d=d):
                    if arrive:
                        g_arrived(j, me + 2 * d)
                    act(g_side_copy(j, me + 2 * d))

        def beside(j, act, arrive):
            if arrive:
                g_arrived(j, side)
            if j in DETOUR:
                @pl.when(z + 1 < length)
                def _():
                    act(g_line_copy(j, side, 1))

                @pl.when(z == 1)
                def _():
                    act(g_line_copy(j, side, -1))

        def start(copy):
            copy.start()

        def sent(copy):
            copy.wait_send()

        def piece_here(j):
            for k in range(length):
                b = 2 * k + (1 - y)

                @pl.when(b != side)
                def _():
                    g_arrived(j, b)

        count = len(pieces)

        def own_all():
            for j in range(count):
                own_low(j, start)
            for d in (1, 2):
                @pl.when(z + d < length)
                def _(d=d):
                    pl.semaphore_wait(ready.at[d - 1], 1)
                for j in range(count):
                    own_up(j, d, start)

        even = lax.rem(s, 2) == 0
        p_down(start)

        @pl.when(even)
        def _():
            own_all()

    for c in range(CHUNKS):
        @pl.when(s < last)
        def _(c=c):
            x_copy(warm_ref.at[:, rows(c), :], 0, c).start()
        k_copy(warm_ref.at[:, rows(c), :], 0, c).start()

    if gathered:
        loads[3].wait()
    for copy in loads[4:]:
        copy.wait()
    cin[...] = jnp.zeros_like(cin)
    cout[...] = jnp.zeros_like(cout)
    levels = cin_ref.shape[0]
    cin[0:levels, :] = cin_ref[...].astype(F32)
    cout[0:levels, :] = cout_ref[...].astype(F32)
    lat[...] = jnp.zeros_like(lat)
    lat[0:levels, :] = lat_ref[...]
    turned = lat[...].T
    lat[...] = turned
    latin[0] = turned.astype(BF16)
    which = lax.broadcasted_iota(jnp.int32, (16, 128), 0)
    times = jnp.zeros((16, 128), F32)
    for i in range(steps + 1):
        times = jnp.where(which == i, ts_ref[i].astype(F32), times)
    bar = jnp.cos((times / 1000.0 + 0.008) / 1.008 * (math.pi / 2)) ** 2
    roots[...] = jnp.sqrt(bar)
    rests[...] = jnp.sqrt(1.0 - bar)
    half = channels // 2
    lane = lax.broadcasted_iota(jnp.int32, (16, channels), 1)
    wave = jnp.where(lane < half, lane, lane - half).astype(F32)
    frequency = jnp.exp(-math.log(10000.0) * wave / half)
    angles = jnp.concatenate([times] * (channels // 128), axis=1) * frequency
    waves = jnp.where(lane < half, jnp.cos(angles), jnp.sin(angles))
    embedded = (waves * (1.0 / (1.0 + jnp.exp(-waves)))).astype(BF16)
    loads[0].wait()
    tv[...] = jnp.dot(embedded, time_w[...], preferred_element_type=F32)

    if gathered:
        cond[...] = prompts_ref[...]

    def front(i, c, parts=False):
        @pl.when(s == 0)
        def _():
            @pl.when(i > 0)
            def _():
                l_copy(i, c).wait_recv()
            first = jnp.dot(latin[i, rows(c), :], cin[...].astype(BF16), preferred_element_type=F32).astype(BF16)
            xbuf[i, 0, rows(c), :] = first
            xbuf[i, 1, rows(c), :] = first

        @pl.when(s > 0)
        def _():
            if parts:
                if c == 0:
                    for j in range(final_piece):
                        x_part(j).wait_recv()
                x_part(final_piece, c).wait_recv()
            else:
                x_copy(ybuf.at[i, :, rows(c), :], i, c).wait_recv()

        if parts:
            if c == 0:
                for j in range(final_piece):
                    k_part(j).wait_recv()
            k_part(final_piece, c).wait_recv()
        else:
            k_copy(ybuf.at[i, :, rows(c), :], i, c).wait_recv()
        time_vec = tv[pl.ds(i, 1), :]
        for g in range(2):
            a = 0.5 * (xbuf[i, g, rows(c), :].astype(F32) + kbuf[i, g, rows(c), :].astype(F32)) + time_vec
            if g == 0:
                a = a + cond[...]
            a_scr[c, g * part:(g + 1) * part, :] = a
        a = a_scr[c]
        normed = (a * lax.rsqrt(jnp.mean(a * a, axis=-1, keepdims=True) + 1e-6)).astype(BF16)
        tile = 256 if hidden % 256 == 0 else hidden
        for j in range(0, hidden, tile):
            gate = jnp.dot(normed, w_in[:, hidden + j:hidden + j + tile], preferred_element_type=F32)
            value = jnp.dot(normed, w_in[:, j:j + tile], preferred_element_type=F32)
            gelu = 0.5 * gate * (1.0 + lax.erf(gate * math.sqrt(0.5)))
            h_scr[c, :, j:j + tile] = (value * gelu).astype(BF16)

    def back(i, c):
        out = (a_scr[c] + jnp.dot(h_scr[c], w_all[...], preferred_element_type=F32)).astype(BF16)

        @pl.when(i < steps - 1)
        def _():
            ybuf[i + 1, :, rows(c), :] = out.reshape(2, part, channels)

            @pl.when(s < last)
            def _():
                x_copy(ybuf.at[i + 1, :, rows(c), :], i + 1, c).start()
            k_copy(ybuf.at[i + 1, :, rows(c), :], i + 1, c).start()

        @pl.when(i == steps - 1)
        def _():
            oseg_ref[:, rows(c), :] = out.reshape(2, part, channels)
        denoise(i, c, out)

    def back_piece(j, c):
        at, width = pieces[j]
        out = a_scr[c, :, at:at + width] + jnp.dot(h_scr[c], w_all[:, at:at + width], preferred_element_type=F32)
        ybuf[1, :, rows(c), at:at + width] = out.astype(BF16).reshape(2, part, width)

    def send_piece(j, c=None):
        @pl.when(s < last)
        def _():
            x_part(j, c).start()
        k_part(j, c).start()

    def denoise(i, c, out):
        @pl.when(s == last)
        def _():
            v = out.astype(F32)
            v = v * lax.rsqrt(jnp.mean(v * v, axis=-1, keepdims=True) + 1e-6)
            m = (v * (1.0 / (1.0 + jnp.exp(-v)))).astype(BF16)
            e = lax.dot_general(m, cout[...].astype(BF16), (((1,), (1,)), ((), ())), preferred_element_type=F32)
            guided = e[part:] + guidance_scale * (e[:part] - e[part:])
            root_now, root_next = roots[pl.ds(i, 1), :], roots[pl.ds(i + 1, 1), :]
            rest_now, rest_next = rests[pl.ds(i, 1), :], rests[pl.ds(i + 1, 1), :]
            clean = (lat[rows(c), :] - rest_now * guided) / root_now
            new = root_next * clean + rest_next * guided
            lat[rows(c), :] = new

            @pl.when(i < steps - 1)
            def _():
                latout[i + 1, rows(c), :] = new.astype(BF16)
                l_copy(i + 1, c).start()

    def back_pieces(j):
        for c in range(CHUNKS):
            back_piece(j, c)
            if j == final_piece:
                send_piece(j, c)
                denoise(0, c, ybuf[1, :, rows(c), :].reshape(2 * part, channels))
        if j < final_piece:
            send_piece(j)

    def fronts(c):
        if c == 0:
            loads[1].wait()
        front(0, c)

    if gathered:
        for c in range(CHUNKS):
            fronts(c)
        loads[2].wait()
        for j in range(len(pieces)):
            back_pieces(j)
    else:
        def go():
            @pl.when(even)
            def _():
                pl.semaphore_signal(turn, inc=1, device_id={"sect": s + 1}, device_id_type=MESH)

            @pl.when(jnp.logical_not(even))
            def _():
                pl.semaphore_wait(turn, 1)
                own_all()

        def stage(t):
            if t < count:
                near(t, start, True)
                beside(t, start, True)
            if 0 <= t - 1 < count:
                middle(t - 1, start, True)
            if 0 <= t - 2 < count:
                far(t - 2, start, True)

        for t in range(LEAD):
            @pl.when(even)
            def _(t=t):
                stage(t)
        go()
        for t in range(LEAD):
            @pl.when(jnp.logical_not(even))
            def _(t=t):
                stage(t)

        @pl.when(z + 1 < length)
        def _():
            pl.semaphore_wait(ready.at[2], 2 * (length - 1 - z))
        p_up(start)
        for t in range(LEAD, 4):
            stage(t)
        for d in range(1, batches):
            b = lax.rem(me + d, batches)
            pltpu.make_async_copy(ptab.at[b], ptab.at[b], p_recv.at[b]).wait()
        cond[...] = ptab[assign_ref[0]]
        fronts(0)
        for t in range(4, 6):
            stage(t)
        for c in range(1, CHUNKS):
            fronts(c)
        for t in range(6, count + 2):
            stage(t)
        loads[2].wait()
        for j in range(count):
            piece_here(j)
            back_pieces(j)
    for c in range(CHUNKS):
        front(1, c, True)
        back(1, c)

    def body(i, carry):
        for c in range(CHUNKS):
            front(i, c)
            back(i, c)
        return carry

    lax.fori_loop(2, steps, body, 0)

    @pl.when(s == last)
    def _():
        turned = lat[...].T
        here = olat_ref.shape[0]
        for d in range(sects):
            fin[d] = turned[d * here:(d + 1) * here, :]
        for d in range(sects - 1):
            f_copy(d).start()
        olat_ref[...] = fin[last]
        for d in range(sects - 1):
            f_copy(d).wait_send()
        for i in range(1, steps):
            for c in range(CHUNKS):
                l_copy(i, c).wait_send()

    @pl.when(s < last)
    def _():
        f_copy(0).wait_recv()
        olat_ref[...] = fin_in[...]
        for c in range(CHUNKS):
            for i in range(steps):
                if i == 1:
                    x_part(final_piece, c).wait_send()
                else:
                    x_copy(ybuf.at[i, :, rows(c), :], i, c).wait_send()
        for j in range(final_piece):
            x_part(j).wait_send()

    for c in range(CHUNKS):
        for i in range(steps):
            if i == 1:
                k_part(final_piece, c).wait_send()
            else:
                k_copy(ybuf.at[i, :, rows(c), :], i, c).wait_send()
    for j in range(final_piece):
        k_part(j).wait_send()
    if not gathered:
        p_down(sent)
        p_up(sent)
        for j in range(count):
            own_low(j, sent)
            for d in (1, 2):
                own_up(j, d, sent)
            for part_of in (near, middle, far, beside):
                part_of(j, sent, False)


def on_device(
    sects, batches, warm, latents, timesteps, assign, prompts, w_in, time_w, w_out, conv_in_w, conv_out_w
):
    positions = latents.shape[1]
    channels = warm.shape[1]
    hidden = w_out.shape[0] * batches
    steps = timesteps.shape[0] - 1
    gathered = w_out.shape[0] % 16 != 0 or batches != 8 or sects != 4
    if gathered:
        w_out = lax.all_gather(w_out, "batch", axis=0, tiled=True)
        table = lax.all_gather(prompts, "batch", axis=0, tiled=True)
        prompts = lax.dynamic_slice_in_dim(table, assign[0], 1, 0).astype(F32)
    whole = pl.BlockSpec(memory_space=pltpu.VMEM)
    apart = pl.BlockSpec(memory_space=pltpu.HBM)
    here = latents.shape[0] // sects
    pieces = len(column_pieces(channels))
    dma = pltpu.SemaphoreType.DMA
    slots = 1 if gathered else batches
    width = 2 * positions // CHUNKS
    segment, final = pl.pallas_call(
        functools.partial(kernel, sects, batches, gathered),
        out_shape=(
            jax.ShapeDtypeStruct((2, positions, channels), BF16),
            jax.ShapeDtypeStruct((here, positions), F32),
        ),
        in_specs=[apart] * 10,
        out_specs=(whole, whole),
        scratch_shapes=[
            pltpu.SMEM(timesteps.shape, jnp.int32),
            pltpu.SMEM(assign.shape, jnp.int32),
            pltpu.VMEM(latents.shape, F32),
            pltpu.VMEM(prompts.shape, prompts.dtype),
            pltpu.VMEM(conv_in_w.shape, BF16),
            pltpu.VMEM(conv_out_w.shape, BF16),
            pltpu.VMEM(w_in.shape, BF16),
            pltpu.VMEM(time_w.shape, BF16),
            pltpu.VMEM((hidden, channels), BF16),
            pltpu.VMEM((steps, 2, positions, channels), BF16),
            pltpu.VMEM((steps, 2, positions, channels), BF16),
            pltpu.VMEM((steps, 2, positions, channels), BF16),
            pltpu.VMEM((CHUNKS, width, channels), F32),
            pltpu.VMEM((CHUNKS, width, hidden), BF16),
            pltpu.VMEM((16, channels), F32),
            pltpu.VMEM((16, 128), F32),
            pltpu.VMEM((16, 128), F32),
            pltpu.VMEM((1, channels), F32),
            pltpu.VMEM((batches, 1, channels), F32),
            pltpu.VMEM((128, channels), F32),
            pltpu.VMEM((128, channels), F32),
            pltpu.VMEM((128, positions), F32),
            pltpu.VMEM((steps, positions, 128), BF16),
            pltpu.VMEM((steps, positions, 128), BF16),
            pltpu.VMEM((sects, here, positions), F32),
            pltpu.VMEM((here, positions), F32),
            pltpu.SemaphoreType.REGULAR((3,)), pltpu.SemaphoreType.REGULAR,
            dma((9,)),
            dma((steps, CHUNKS)), dma((steps, CHUNKS)),
            dma((steps, CHUNKS)), dma((steps, CHUNKS)),
            dma((steps, CHUNKS)), dma((steps, CHUNKS)),
            dma((sects,)), dma(()),
            dma((slots,)), dma((slots,)),
            dma((4, pieces, slots)), dma((pieces, slots)), dma((pieces, slots)),
            dma((pieces,)), dma((pieces,)), dma((pieces,)), dma((pieces,)),
        ],
        compiler_params=pltpu.CompilerParams(
            collective_id=0, has_side_effects=True, vmem_limit_bytes=60 * 1024 * 1024
        ),
    )(
        timesteps, assign, warm.reshape(2, positions, channels), latents, prompts,
        w_in, time_w, w_out, conv_in_w, conv_out_w,
    )
    return segment.reshape(2 * positions, channels), final


def solution(mesh):
    return jax.shard_map(
        functools.partial(on_device, mesh.shape["sect"], mesh.shape["batch"]),
        mesh=mesh,
        in_specs=(
            P(("sect", "batch"), None),
            P(None, "batch"),
            P(),
            P("batch"),
            P("batch", None),
            P("sect", None),
            P("sect", None),
            P(("sect", "batch"), None),
            P(),
            P(),
        ),
        out_specs=(P(("sect", "batch"), None), P("sect", "batch")),
        check_vma=False,
    )
```

```python
import functools
import math

import jax
import jax.numpy as jnp
from jax import lax
from jax.experimental import pallas as pl
from jax.experimental.pallas import tpu as pltpu
from jax.sharding import PartitionSpec as P

guidance_scale = 3.0
MESH = pl.DeviceIdType.MESH
F32 = jnp.float32
BF16 = jnp.bfloat16
CHUNKS = 2
SPLIT = (128, 128, 128, 128, 128)
DETOUR = (3, 4)
LEAD = 0
LAG = 5
BLAG = 10
FRONTS = (9, 12)


def column_pieces(channels):
    widths = SPLIT if sum(SPLIT) == channels else (channels,)
    return [(sum(widths[:j]), width) for j, width in enumerate(widths)]


def kernel(
    sects, batches, gathered,
    ts_hbm, assign_hbm, warm_ref, lat_hbm, prompts_hbm, w_in_ref, time_w_ref, w_out_ref, cin_hbm, cout_hbm,
    oseg_ref, olat_ref,
    ts_ref, assign_ref, lat_ref, prompts_ref, cin_ref, cout_ref,
    w_in, time_w, w_all, xbuf, kbuf, ybuf, a_scr, h_scr, tv, roots, rests, cond, ptab,
    cin, cout, lat, latin, latout, fin, fin_in,
    ready, turn, load_sem, x_send, x_recv, k_send, k_recv, l_send, l_recv, f_send, f_recv,
    p_send, p_recv, g_line, g_side, g_recv, xc_send, xc_recv, kc_send, kc_recv,
):
    s = lax.axis_index("sect")
    me = lax.axis_index("batch")
    steps = ts_ref.shape[0] - 1
    _, positions, channels = warm_ref.shape
    hidden = w_all.shape[0]
    part = positions // CHUNKS
    up = lax.rem(s + 1, sects)
    down = lax.rem(s + sects - 1, sects)
    last = sects - 1
    pieces = column_pieces(channels)
    final_piece = len(pieces) - 1

    loads = [
        pltpu.make_async_copy(time_w_ref, time_w, load_sem.at[0]),
        pltpu.make_async_copy(w_in_ref, w_in, load_sem.at[1]),
    ]
    if gathered:
        loads.append(pltpu.make_async_copy(w_out_ref, w_all, load_sem.at[2]))
    else:
        depth = w_out_ref.shape[0]
        own_rows = pl.ds(pl.multiple_of(me * depth, depth), depth)
        loads.append(pltpu.make_async_copy(w_out_ref, w_all.at[own_rows], load_sem.at[2]))
    pairs = [(prompts_hbm, prompts_ref), (ts_hbm, ts_ref), (assign_hbm, assign_ref), (lat_hbm, lat_ref),
             (cin_hbm, cin_ref), (cout_hbm, cout_ref)]
    for j, (src, dst) in enumerate(pairs):
        loads.append(pltpu.make_async_copy(src, dst, load_sem.at[3 + j]))
    for copy in loads[3:] + loads[:3]:
        copy.start()

    barrier = pltpu.get_barrier_semaphore()
    for d in range(1, sects):
        pl.semaphore_signal(barrier, inc=1, device_id={"sect": lax.rem(s + d, sects)}, device_id_type=MESH)
    met = sects - 1
    if not gathered:
        z, y = me // 2, lax.rem(me, 2)
        length = batches // 2
        side = z * 2 + (1 - y)
        pl.semaphore_signal(barrier, inc=1, device_id={"batch": side}, device_id_type=MESH)
        for d in range(1, length):
            @pl.when(z + d < length)
            def _(d=d):
                for b in (me + 2 * d, side + 2 * d):
                    pl.semaphore_signal(barrier, inc=1, device_id={"batch": b}, device_id_type=MESH)
        met = met + 1 + 2 * z
        loads[3].wait()
        ptab[me] = prompts_ref[...].astype(F32)
    pl.semaphore_wait(barrier, met)
    if not gathered:
        for d in range(1, length):
            @pl.when(z >= d)
            def _(d=d):
                for b in (me - 2 * d, side - 2 * d):
                    pl.semaphore_signal(ready.at[1], inc=1, device_id={"batch": b}, device_id_type=MESH)
                if d == 1:
                    pl.semaphore_signal(ready.at[0], inc=1, device_id={"batch": me - 2 * d}, device_id_type=MESH)

    def rows(c):
        return pl.ds(c * part, part)

    def x_copy(src, slot, c):
        return pltpu.make_async_remote_copy(
            src_ref=src, dst_ref=xbuf.at[slot, :, rows(c), :], send_sem=x_send.at[slot, c],
            recv_sem=x_recv.at[slot, c], device_id={"sect": up}, device_id_type=MESH)

    def k_copy(src, slot, c):
        return pltpu.make_async_remote_copy(
            src_ref=src, dst_ref=kbuf.at[slot, :, rows(c), :], send_sem=k_send.at[slot, c],
            recv_sem=k_recv.at[slot, c], device_id={"sect": down}, device_id_type=MESH)

    def columns(ref, j, c=None):
        at, width = pieces[j]
        return ref.at[1, :, slice(None) if c is None else rows(c), pl.ds(at, width)]

    def x_part(j, c=None):
        sems = (xc_send.at[j], xc_recv.at[j]) if c is None else (x_send.at[1, c], x_recv.at[1, c])
        return pltpu.make_async_remote_copy(
            src_ref=columns(ybuf, j, c), dst_ref=columns(xbuf, j, c), send_sem=sems[0],
            recv_sem=sems[1], device_id={"sect": up}, device_id_type=MESH)

    def k_part(j, c=None):
        sems = (kc_send.at[j], kc_recv.at[j]) if c is None else (k_send.at[1, c], k_recv.at[1, c])
        return pltpu.make_async_remote_copy(
            src_ref=columns(ybuf, j, c), dst_ref=columns(kbuf, j, c), send_sem=sems[0],
            recv_sem=sems[1], device_id={"sect": down}, device_id_type=MESH)

    def l_copy(slot, c):
        return pltpu.make_async_remote_copy(
            src_ref=latout.at[slot, rows(c), :], dst_ref=latin.at[slot, rows(c), :], send_sem=l_send.at[slot, c],
            recv_sem=l_recv.at[slot, c], device_id={"sect": 0}, device_id_type=MESH)

    def f_copy(d):
        return pltpu.make_async_remote_copy(
            src_ref=fin.at[d], dst_ref=fin_in, send_sem=f_send.at[d],
            recv_sem=f_recv, device_id={"sect": d}, device_id_type=MESH)

    if not gathered:
        def p_copy(b):
            return pltpu.make_async_remote_copy(
                src_ref=ptab.at[me], dst_ref=ptab.at[me], send_sem=p_send.at[b], recv_sem=p_recv.at[me],
                device_id={"batch": b}, device_id_type=MESH)

        def p_down(act):
            act(p_copy(side))
            for d in range(1, length):
                @pl.when(z >= d)
                def _(d=d):
                    act(p_copy(me - 2 * d))
                    act(p_copy(side - 2 * d))

        def p_up(act):
            for d in range(1, length):
                @pl.when(z + d < length)
                def _(d=d):
                    act(p_copy(me + 2 * d))
                    act(p_copy(side + 2 * d))

        def block(j, b):
            at, width = pieces[j]
            return w_all.at[pl.ds(pl.multiple_of(b * depth, depth), depth), pl.ds(at, width)]

        def g_copy(j, b, to, sem, own):
            at, width = pieces[j]
            return pltpu.make_async_remote_copy(
                src_ref=w_out_ref.at[:, pl.ds(at, width)] if own else block(j, b), dst_ref=block(j, b), send_sem=sem,
                recv_sem=g_recv.at[j, b], device_id={"batch": to}, device_id_type=MESH)

        def g_line_copy(j, b, d, own=False):
            return g_copy(j, b, me + 2 * d, g_line.at[0 if d > 0 else 1, j, b], own)

        def g_side_copy(j, b, own=False):
            return g_copy(j, b, side, g_side.at[j, b], own)

        def g_arrived(j, b):
            pltpu.make_async_copy(block(j, b), block(j, b), g_recv.at[j, b]).wait()

        def own_side(j, act):
            act(g_side_copy(j, me, True))

        def own_line(j, d, act):
            @pl.when((z + d < length) & (z + d >= 0))
            def _():
                act(g_line_copy(j, me, d, True))

        def passed(j, k, act, arrive, dirs=(1, -1)):
            detour = j in DETOUR and k == 1
            for d in dirs:
                @pl.when((z + d * k < length) & (z + d * k >= 0))
                def _(d=d):
                    b = me + 2 * d * k
                    if arrive:
                        g_arrived(j, b)

                    @pl.when((z - d < length) & (z - d >= 0))
                    def _():
                        act(g_line_copy(j, b, -d))
                    if not detour:
                        act(g_side_copy(j, b))
                    elif d > 0:
                        @pl.when(z > 0)
                        def _():
                            act(g_side_copy(j, b))

        def beside(j, act, arrive):
            if arrive:
                g_arrived(j, side)
            if j in DETOUR:
                @pl.when(z + 1 < length)
                def _():
                    act(g_line_copy(j, side, 1))

                @pl.when(z == 1)
                def _():
                    act(g_line_copy(j, side, -1))

        def start(copy):
            copy.start()

        def sent(copy):
            copy.wait_send()

        def piece_here(j):
            for k in range(length):
                b = 2 * k + (1 - y)

                if j not in DETOUR:
                    g_arrived(j, b)
                else:
                    @pl.when(b != side)
                    def _():
                        g_arrived(j, b)

        count = len(pieces)

        def own_all():
            for j in range(count):
                own_line(j, -1, start)
                own_side(j, start)

            @pl.when(z + 1 < length)
            def _():
                pl.semaphore_wait(ready.at[0], 1)
            for j in range(count):
                own_line(j, 1, start)

        even = lax.rem(s, 2) == 0
        p_down(start)

        @pl.when(even)
        def _():
            own_all()

    for c in range(CHUNKS):
        @pl.when(s < last)
        def _(c=c):
            x_copy(warm_ref.at[:, rows(c), :], 0, c).start()
        k_copy(warm_ref.at[:, rows(c), :], 0, c).start()

    if gathered:
        loads[3].wait()
    for copy in loads[4:]:
        copy.wait()
    cin[...] = jnp.zeros_like(cin)
    cout[...] = jnp.zeros_like(cout)
    levels = cin_ref.shape[0]
    cin[0:levels, :] = cin_ref[...].astype(F32)
    cout[0:levels, :] = cout_ref[...].astype(F32)
    lat[...] = jnp.zeros_like(lat)
    lat[0:levels, :] = lat_ref[...]
    turned = lat[...].T
    lat[...] = turned
    latin[0] = turned.astype(BF16)
    which = lax.broadcasted_iota(jnp.int32, (16, 128), 0)
    times = jnp.zeros((16, 128), F32)
    for i in range(steps + 1):
        times = jnp.where(which == i, ts_ref[i].astype(F32), times)
    bar = jnp.cos((times / 1000.0 + 0.008) / 1.008 * (math.pi / 2)) ** 2
    roots[...] = jnp.sqrt(bar)
    rests[...] = jnp.sqrt(1.0 - bar)
    half = channels // 2
    lane = lax.broadcasted_iota(jnp.int32, (16, channels), 1)
    wave = jnp.where(lane < half, lane, lane - half).astype(F32)
    frequency = jnp.exp(-math.log(10000.0) * wave / half)
    angles = jnp.concatenate([times] * (channels // 128), axis=1) * frequency
    waves = jnp.where(lane < half, jnp.cos(angles), jnp.sin(angles))
    embedded = (waves * (1.0 / (1.0 + jnp.exp(-waves)))).astype(BF16)
    loads[0].wait()
    tv[...] = jnp.dot(embedded, time_w[...], preferred_element_type=F32)

    if gathered:
        cond[...] = prompts_ref[...]

    def front(i, c, parts=False):
        @pl.when(s == 0)
        def _():
            @pl.when(i > 0)
            def _():
                l_copy(i, c).wait_recv()
            first = jnp.dot(latin[i, rows(c), :], cin[...].astype(BF16), preferred_element_type=F32).astype(BF16)
            xbuf[i, 0, rows(c), :] = first
            xbuf[i, 1, rows(c), :] = first

        @pl.when(s > 0)
        def _():
            if parts:
                if c == 0:
                    for j in range(final_piece):
                        x_part(j).wait_recv()
                x_part(final_piece, c).wait_recv()
            else:
                x_copy(ybuf.at[i, :, rows(c), :], i, c).wait_recv()

        if parts:
            if c == 0:
                for j in range(final_piece):
                    k_part(j).wait_recv()
            k_part(final_piece, c).wait_recv()
        else:
            k_copy(ybuf.at[i, :, rows(c), :], i, c).wait_recv()
        time_vec = tv[pl.ds(i, 1), :]
        for g in range(2):
            a = 0.5 * (xbuf[i, g, rows(c), :].astype(F32) + kbuf[i, g, rows(c), :].astype(F32)) + time_vec
            if g == 0:
                a = a + cond[...]
            a_scr[c, g * part:(g + 1) * part, :] = a
        a = a_scr[c]
        normed = (a * lax.rsqrt(jnp.mean(a * a, axis=-1, keepdims=True) + 1e-6)).astype(BF16)
        tile = 256 if hidden % 256 == 0 else hidden
        for j in range(0, hidden, tile):
            gate = jnp.dot(normed, w_in[:, hidden + j:hidden + j + tile], preferred_element_type=F32)
            value = jnp.dot(normed, w_in[:, j:j + tile], preferred_element_type=F32)
            gelu = 0.5 * gate * (1.0 + lax.erf(gate * math.sqrt(0.5)))
            h_scr[c, :, j:j + tile] = (value * gelu).astype(BF16)

    def back(i, c):
        out = (a_scr[c] + jnp.dot(h_scr[c], w_all[...], preferred_element_type=F32)).astype(BF16)

        @pl.when(i < steps - 1)
        def _():
            ybuf[i + 1, :, rows(c), :] = out.reshape(2, part, channels)

            @pl.when(s < last)
            def _():
                x_copy(ybuf.at[i + 1, :, rows(c), :], i + 1, c).start()
            k_copy(ybuf.at[i + 1, :, rows(c), :], i + 1, c).start()

        @pl.when(i == steps - 1)
        def _():
            oseg_ref[:, rows(c), :] = out.reshape(2, part, channels)
        denoise(i, c, out)

    def back_piece(j, c):
        at, width = pieces[j]
        out = a_scr[c, :, at:at + width] + jnp.dot(h_scr[c], w_all[:, at:at + width], preferred_element_type=F32)
        ybuf[1, :, rows(c), at:at + width] = out.astype(BF16).reshape(2, part, width)

    def send_piece(j, c=None):
        @pl.when(s < last)
        def _():
            x_part(j, c).start()
        k_part(j, c).start()

    def denoise(i, c, out):
        @pl.when(s == last)
        def _():
            v = out.astype(F32)
            v = v * lax.rsqrt(jnp.mean(v * v, axis=-1, keepdims=True) + 1e-6)
            m = (v * (1.0 / (1.0 + jnp.exp(-v)))).astype(BF16)
            e = lax.dot_general(m, cout[...].astype(BF16), (((1,), (1,)), ((), ())), preferred_element_type=F32)
            guided = e[part:] + guidance_scale * (e[:part] - e[part:])
            root_now, root_next = roots[pl.ds(i, 1), :], roots[pl.ds(i + 1, 1), :]
            rest_now, rest_next = rests[pl.ds(i, 1), :], rests[pl.ds(i + 1, 1), :]
            clean = (lat[rows(c), :] - rest_now * guided) / root_now
            new = root_next * clean + rest_next * guided
            lat[rows(c), :] = new

            @pl.when(i < steps - 1)
            def _():
                latout[i + 1, rows(c), :] = new.astype(BF16)
                l_copy(i + 1, c).start()

    def back_pieces(j):
        for c in range(CHUNKS):
            back_piece(j, c)
            if j == final_piece:
                send_piece(j, c)
                denoise(0, c, ybuf[1, :, rows(c), :].reshape(2 * part, channels))
        if j < final_piece:
            send_piece(j)

    def fronts(c):
        if c == 0:
            loads[1].wait()
        front(0, c)

    if gathered:
        for c in range(CHUNKS):
            fronts(c)
        loads[2].wait()
        for j in range(len(pieces)):
            back_pieces(j)
    else:
        def go():
            @pl.when(even)
            def _():
                pl.semaphore_signal(turn, inc=1, device_id={"sect": s + 1}, device_id_type=MESH)

            @pl.when(jnp.logical_not(even))
            def _():
                pl.semaphore_wait(turn, 1)
                own_all()

        def stage(t):
            for k in (1, 2, 3):
                j = t - (k - 1) * LAG
                if 0 <= j < count:
                    passed(j, k, start, True)
            j = t - BLAG
            if j in DETOUR and j < count:
                beside(j, start, True)

        for t in range(LEAD):
            @pl.when(even)
            def _(t=t):
                stage(t)
        go()
        for t in range(LEAD):
            @pl.when(jnp.logical_not(even))
            def _(t=t):
                stage(t)

        @pl.when(z + 1 < length)
        def _():
            pl.semaphore_wait(ready.at[1], 2 * (length - 1 - z))
        p_up(start)
        for t in range(LEAD, FRONTS[0]):
            stage(t)
        for d in range(1, batches):
            b = lax.rem(me + d, batches)
            pltpu.make_async_copy(ptab.at[b], ptab.at[b], p_recv.at[b]).wait()
        cond[...] = ptab[assign_ref[0]]
        fronts(0)
        for t in range(FRONTS[0], FRONTS[1]):
            stage(t)
        for c in range(1, CHUNKS):
            fronts(c)
        for t in range(FRONTS[1], max(2 * LAG, BLAG) + count):
            stage(t)
        loads[2].wait()
        for j in range(count):
            piece_here(j)
            back_pieces(j)
    for c in range(CHUNKS):
        front(1, c, True)
        back(1, c)

    def body(i, carry):
        for c in range(CHUNKS):
            front(i, c)
            back(i, c)
        return carry

    lax.fori_loop(2, steps, body, 0)

    @pl.when(s == last)
    def _():
        turned = lat[...].T
        here = olat_ref.shape[0]
        for d in range(sects):
            fin[d] = turned[d * here:(d + 1) * here, :]
        for d in range(sects - 1):
            f_copy(d).start()
        olat_ref[...] = fin[last]
        for d in range(sects - 1):
            f_copy(d).wait_send()
        for i in range(1, steps):
            for c in range(CHUNKS):
                l_copy(i, c).wait_send()

    @pl.when(s < last)
    def _():
        f_copy(0).wait_recv()
        olat_ref[...] = fin_in[...]
        for c in range(CHUNKS):
            for i in range(steps):
                if i == 1:
                    x_part(final_piece, c).wait_send()
                else:
                    x_copy(ybuf.at[i, :, rows(c), :], i, c).wait_send()
        for j in range(final_piece):
            x_part(j).wait_send()

    for c in range(CHUNKS):
        for i in range(steps):
            if i == 1:
                k_part(final_piece, c).wait_send()
            else:
                k_copy(ybuf.at[i, :, rows(c), :], i, c).wait_send()
    for j in range(final_piece):
        k_part(j).wait_send()
    if not gathered:
        p_down(sent)
        p_up(sent)
        for j in range(count):
            own_side(j, sent)
            for d in (1, -1):
                own_line(j, d, sent)
            for k in (1, 2, 3):
                passed(j, k, sent, False)
            beside(j, sent, False)


def hand_over(segment_ref, final_ref, oseg_ref, olat_ref):
    oseg_ref[...] = segment_ref[...]
    olat_ref[...] = final_ref[...]


def on_device(
    sects, batches, warm, latents, timesteps, assign, prompts, w_in, time_w, w_out, conv_in_w, conv_out_w
):
    positions = latents.shape[1]
    channels = warm.shape[1]
    hidden = w_out.shape[0] * batches
    steps = timesteps.shape[0] - 1
    gathered = w_out.shape[0] % 16 != 0 or batches != 8 or sects != 4
    if gathered:
        w_out = lax.all_gather(w_out, "batch", axis=0, tiled=True)
        table = lax.all_gather(prompts, "batch", axis=0, tiled=True)
        prompts = lax.dynamic_slice_in_dim(table, assign[0], 1, 0).astype(F32)
    whole = pl.BlockSpec(memory_space=pltpu.VMEM)
    apart = pl.BlockSpec(memory_space=pltpu.HBM)
    here = latents.shape[0] // sects
    pieces = len(column_pieces(channels))
    dma = pltpu.SemaphoreType.DMA
    slots = 1 if gathered else batches
    width = 2 * positions // CHUNKS
    segment, final = pl.pallas_call(
        functools.partial(kernel, sects, batches, gathered),
        out_shape=(
            pltpu.VMEM((2, positions, channels), BF16),
            pltpu.VMEM((here, positions), F32),
        ),
        in_specs=[apart] * 10,
        out_specs=(whole, whole),
        scratch_shapes=[
            pltpu.SMEM(timesteps.shape, jnp.int32),
            pltpu.SMEM(assign.shape, jnp.int32),
            pltpu.VMEM(latents.shape, F32),
            pltpu.VMEM(prompts.shape, prompts.dtype),
            pltpu.VMEM(conv_in_w.shape, BF16),
            pltpu.VMEM(conv_out_w.shape, BF16),
            pltpu.VMEM(w_in.shape, BF16),
            pltpu.VMEM(time_w.shape, BF16),
            pltpu.VMEM((hidden, channels), BF16),
            pltpu.VMEM((steps, 2, positions, channels), BF16),
            pltpu.VMEM((steps, 2, positions, channels), BF16),
            pltpu.VMEM((steps, 2, positions, channels), BF16),
            pltpu.VMEM((CHUNKS, width, channels), F32),
            pltpu.VMEM((CHUNKS, width, hidden), BF16),
            pltpu.VMEM((16, channels), F32),
            pltpu.VMEM((16, 128), F32),
            pltpu.VMEM((16, 128), F32),
            pltpu.VMEM((1, channels), F32),
            pltpu.VMEM((batches, 1, channels), F32),
            pltpu.VMEM((128, channels), F32),
            pltpu.VMEM((128, channels), F32),
            pltpu.VMEM((128, positions), F32),
            pltpu.VMEM((steps, positions, 128), BF16),
            pltpu.VMEM((steps, positions, 128), BF16),
            pltpu.VMEM((sects, here, positions), F32),
            pltpu.VMEM((here, positions), F32),
            pltpu.SemaphoreType.REGULAR((2,)), pltpu.SemaphoreType.REGULAR,
            dma((9,)),
            dma((steps, CHUNKS)), dma((steps, CHUNKS)),
            dma((steps, CHUNKS)), dma((steps, CHUNKS)),
            dma((steps, CHUNKS)), dma((steps, CHUNKS)),
            dma((sects,)), dma(()),
            dma((slots,)), dma((slots,)),
            dma((2, pieces, slots)), dma((pieces, slots)), dma((pieces, slots)),
            dma((pieces,)), dma((pieces,)), dma((pieces,)), dma((pieces,)),
        ],
        compiler_params=pltpu.CompilerParams(
            collective_id=0, has_side_effects=True, vmem_limit_bytes=58000 * 1024
        ),
    )(
        timesteps, assign, warm.reshape(2, positions, channels), latents, prompts,
        w_in, time_w, w_out, conv_in_w, conv_out_w,
    )
    return pl.pallas_call(
        hand_over,
        out_shape=(
            jax.ShapeDtypeStruct((2 * positions, channels), BF16),
            jax.ShapeDtypeStruct((here, positions), F32),
        ),
        in_specs=[whole, whole],
        out_specs=(whole, whole),
        compiler_params=pltpu.CompilerParams(vmem_limit_bytes=4 * 1024 * 1024),
    )(segment.reshape(2 * positions, channels), final)


def solution(mesh):
    return jax.shard_map(
        functools.partial(on_device, mesh.shape["sect"], mesh.shape["batch"]),
        mesh=mesh,
        in_specs=(
            P(("sect", "batch"), None),
            P(None, "batch"),
            P(),
            P("batch"),
            P("batch", None),
            P("sect", None),
            P("sect", None),
            P(("sect", "batch"), None),
            P(),
            P(),
        ),
        out_specs=(P(("sect", "batch"), None), P("sect", "batch")),
        check_vma=False,
    )
```

```python
import functools
import math

import jax
import jax.numpy as jnp
from jax import lax
from jax.experimental import pallas as pl
from jax.experimental.pallas import tpu as pltpu
from jax.sharding import PartitionSpec as P

guidance_scale = 3.0
MESH = pl.DeviceIdType.MESH
F32 = jnp.float32
BF16 = jnp.bfloat16
CHUNKS = 2
SPLIT = (128, 128, 128, 128, 128)
DETOUR = (3, 4)
LEAD = 4
LAG = 5
BLAG = 10
OFFSET = 1
FRONTS = (9, 12)


def column_pieces(channels):
    widths = SPLIT if sum(SPLIT) == channels else (channels,)
    return [(sum(widths[:j]), width) for j, width in enumerate(widths)]


def kernel(
    sects, batches, gathered,
    ts_hbm, assign_hbm, warm_ref, lat_hbm, prompts_hbm, w_in_ref, time_w_ref, w_out_ref, cin_hbm, cout_hbm,
    oseg_ref, olat_ref,
    ts_ref, assign_ref, lat_ref, prompts_ref, cin_ref, cout_ref,
    w_in, time_w, w_all, xbuf, kbuf, ybuf, a_scr, h_scr, tv, roots, rests, cond, ptab,
    cin, cout, lat, latin, latout, fin, fin_in,
    ready, turn, passage, load_sem, x_send, x_recv, k_send, k_recv, l_send, l_recv, f_send, f_recv,
    p_send, p_recv, g_line, g_side, g_recv, xc_send, xc_recv, kc_send, kc_recv,
):
    s = lax.axis_index("sect")
    me = lax.axis_index("batch")
    steps = ts_ref.shape[0] - 1
    _, positions, channels = warm_ref.shape
    hidden = w_all.shape[0]
    part = positions // CHUNKS
    up = lax.rem(s + 1, sects)
    down = lax.rem(s + sects - 1, sects)
    last = sects - 1
    pieces = column_pieces(channels)
    final_piece = len(pieces) - 1
    held = steps - 2 if steps >= 4 and sects == 4 else steps

    loads = [
        pltpu.make_async_copy(time_w_ref, time_w, load_sem.at[0]),
        pltpu.make_async_copy(w_in_ref, w_in, load_sem.at[1]),
    ]
    if gathered:
        loads.append(pltpu.make_async_copy(w_out_ref, w_all, load_sem.at[2]))
    else:
        depth = w_out_ref.shape[0]
        own_rows = pl.ds(pl.multiple_of(me * depth, depth), depth)
        loads.append(pltpu.make_async_copy(w_out_ref, w_all.at[own_rows], load_sem.at[2]))
    pairs = [(prompts_hbm, prompts_ref), (ts_hbm, ts_ref), (assign_hbm, assign_ref), (lat_hbm, lat_ref),
             (cin_hbm, cin_ref), (cout_hbm, cout_ref)]
    for j, (src, dst) in enumerate(pairs):
        loads.append(pltpu.make_async_copy(src, dst, load_sem.at[3 + j]))
    for copy in loads[3:] + loads[:3]:
        copy.start()

    barrier = pltpu.get_barrier_semaphore()
    for d in range(1, sects):
        pl.semaphore_signal(barrier, inc=1, device_id={"sect": lax.rem(s + d, sects)}, device_id_type=MESH)
    met = sects - 1
    if not gathered:
        z, y = me // 2, lax.rem(me, 2)
        length = batches // 2
        side = z * 2 + (1 - y)
        pl.semaphore_signal(barrier, inc=1, device_id={"batch": side}, device_id_type=MESH)
        for d in range(1, length):
            @pl.when(z + d < length)
            def _(d=d):
                for b in (me + 2 * d, side + 2 * d):
                    pl.semaphore_signal(barrier, inc=1, device_id={"batch": b}, device_id_type=MESH)
        met = met + 1 + 2 * z
        loads[3].wait()
        ptab[me] = prompts_ref[...].astype(F32)
    pl.semaphore_wait(barrier, met)
    if not gathered:
        for d in range(1, length):
            @pl.when(z >= d)
            def _(d=d):
                for b in (me - 2 * d, side - 2 * d):
                    pl.semaphore_signal(ready.at[1], inc=1, device_id={"batch": b}, device_id_type=MESH)
                if d == 1:
                    pl.semaphore_signal(ready.at[0], inc=1, device_id={"batch": me - 2 * d}, device_id_type=MESH)

    def rows(c):
        return pl.ds(c * part, part)

    def x_copy(src, slot, c):
        return pltpu.make_async_remote_copy(
            src_ref=src, dst_ref=xbuf.at[slot, :, rows(c), :], send_sem=x_send.at[slot, c],
            recv_sem=x_recv.at[slot, c], device_id={"sect": up}, device_id_type=MESH)

    def k_copy(src, slot, c):
        return pltpu.make_async_remote_copy(
            src_ref=src, dst_ref=kbuf.at[slot, :, rows(c), :], send_sem=k_send.at[slot, c],
            recv_sem=k_recv.at[slot, c], device_id={"sect": down}, device_id_type=MESH)

    def columns(ref, j, c=None):
        at, width = pieces[j]
        return ref.at[1, :, slice(None) if c is None else rows(c), pl.ds(at, width)]

    def x_part(j, c=None):
        sems = (xc_send.at[j], xc_recv.at[j]) if c is None else (x_send.at[1, c], x_recv.at[1, c])
        return pltpu.make_async_remote_copy(
            src_ref=columns(ybuf, j, c), dst_ref=columns(xbuf, j, c), send_sem=sems[0],
            recv_sem=sems[1], device_id={"sect": up}, device_id_type=MESH)

    def k_part(j, c=None):
        sems = (kc_send.at[j], kc_recv.at[j]) if c is None else (k_send.at[1, c], k_recv.at[1, c])
        return pltpu.make_async_remote_copy(
            src_ref=columns(ybuf, j, c), dst_ref=columns(kbuf, j, c), send_sem=sems[0],
            recv_sem=sems[1], device_id={"sect": down}, device_id_type=MESH)

    def l_copy(slot, c):
        return pltpu.make_async_remote_copy(
            src_ref=latout.at[slot, rows(c), :], dst_ref=latin.at[slot, rows(c), :], send_sem=l_send.at[slot, c],
            recv_sem=l_recv.at[slot, c], device_id={"sect": 0}, device_id_type=MESH)

    def f_copy(d):
        return pltpu.make_async_remote_copy(
            src_ref=fin.at[d], dst_ref=fin_in, send_sem=f_send.at[d],
            recv_sem=f_recv, device_id={"sect": d}, device_id_type=MESH)

    if not gathered:
        def p_copy(b):
            return pltpu.make_async_remote_copy(
                src_ref=ptab.at[me], dst_ref=ptab.at[me], send_sem=p_send.at[b], recv_sem=p_recv.at[me],
                device_id={"batch": b}, device_id_type=MESH)

        def p_down(act):
            act(p_copy(side))
            for d in range(1, length):
                @pl.when(z >= d)
                def _(d=d):
                    act(p_copy(me - 2 * d))
                    act(p_copy(side - 2 * d))

        def p_up(act):
            for d in range(1, length):
                @pl.when(z + d < length)
                def _(d=d):
                    act(p_copy(me + 2 * d))
                    act(p_copy(side + 2 * d))

        def block(j, b):
            at, width = pieces[j]
            return w_all.at[pl.ds(pl.multiple_of(b * depth, depth), depth), pl.ds(at, width)]

        def g_copy(j, b, to, sem, own):
            at, width = pieces[j]
            return pltpu.make_async_remote_copy(
                src_ref=w_out_ref.at[:, pl.ds(at, width)] if own else block(j, b), dst_ref=block(j, b), send_sem=sem,
                recv_sem=g_recv.at[j, b], device_id={"batch": to}, device_id_type=MESH)

        def g_line_copy(j, b, d, own=False):
            return g_copy(j, b, me + 2 * d, g_line.at[0 if d > 0 else 1, j, b], own)

        def g_side_copy(j, b, own=False):
            return g_copy(j, b, side, g_side.at[j, b], own)

        def g_arrived(j, b):
            pltpu.make_async_copy(block(j, b), block(j, b), g_recv.at[j, b]).wait()

        def own_side(j, act):
            act(g_side_copy(j, me, True))

        def own_line(j, d, act):
            @pl.when((z + d < length) & (z + d >= 0))
            def _():
                act(g_line_copy(j, me, d, True))

        def passed(j, k, act, arrive, dirs=(1, -1)):
            detour = j in DETOUR and k == 1
            for d in dirs:
                @pl.when((z + d * k < length) & (z + d * k >= 0))
                def _(d=d):
                    b = me + 2 * d * k
                    if arrive:
                        g_arrived(j, b)

                    @pl.when((z - d < length) & (z - d >= 0))
                    def _():
                        act(g_line_copy(j, b, -d))
                    if not detour:
                        act(g_side_copy(j, b))
                    elif d > 0:
                        @pl.when(z > 0)
                        def _():
                            act(g_side_copy(j, b))

        def beside(j, act, arrive):
            if arrive:
                g_arrived(j, side)
            if j in DETOUR:
                @pl.when(z + 1 < length)
                def _():
                    act(g_line_copy(j, side, 1))

                @pl.when(z == 1)
                def _():
                    act(g_line_copy(j, side, -1))

        def start(copy):
            copy.start()

        def sent(copy):
            copy.wait_send()

        def piece_here(j):
            for k in range(length):
                b = 2 * k + (1 - y)

                if j not in DETOUR:
                    g_arrived(j, b)
                else:
                    @pl.when(b != side)
                    def _():
                        g_arrived(j, b)

        count = len(pieces)

        def own_all():
            for j in range(count):
                own_line(j, -1, start)
                own_side(j, start)

            @pl.when(z + 1 < length)
            def _():
                pl.semaphore_wait(ready.at[0], 1)
            for j in range(count):
                own_line(j, 1, start)

        even = lax.rem(s, 2) == 0
        p_down(start)

        @pl.when(even)
        def _():
            own_all()

    for c in range(CHUNKS):
        @pl.when(s < last)
        def _(c=c):
            x_copy(warm_ref.at[:, rows(c), :], 0, c).start()
        k_copy(warm_ref.at[:, rows(c), :], 0, c).start()

    if gathered:
        loads[3].wait()
    for copy in loads[4:]:
        copy.wait()
    cin[...] = jnp.zeros_like(cin)
    cout[...] = jnp.zeros_like(cout)
    levels = cin_ref.shape[0]
    cin[0:levels, :] = cin_ref[...].astype(F32)
    cout[0:levels, :] = cout_ref[...].astype(F32)
    lat[...] = jnp.zeros_like(lat)
    lat[0:levels, :] = lat_ref[...]
    turned = lat[...].T
    lat[...] = turned
    latin[0] = turned.astype(BF16)
    which = lax.broadcasted_iota(jnp.int32, (16, 128), 0)
    times = jnp.zeros((16, 128), F32)
    for i in range(steps + 1):
        times = jnp.where(which == i, ts_ref[i].astype(F32), times)
    bar = jnp.cos((times / 1000.0 + 0.008) / 1.008 * (math.pi / 2)) ** 2
    roots[...] = jnp.sqrt(bar)
    rests[...] = jnp.sqrt(1.0 - bar)
    half = channels // 2
    lane = lax.broadcasted_iota(jnp.int32, (16, channels), 1)
    wave = jnp.where(lane < half, lane, lane - half).astype(F32)
    frequency = jnp.exp(-math.log(10000.0) * wave / half)
    angles = jnp.concatenate([times] * (channels // 128), axis=1) * frequency
    waves = jnp.where(lane < half, jnp.cos(angles), jnp.sin(angles))
    embedded = (waves * (1.0 / (1.0 + jnp.exp(-waves)))).astype(BF16)
    loads[0].wait()
    tv[...] = jnp.dot(embedded, time_w[...], preferred_element_type=F32)

    if gathered:
        cond[...] = prompts_ref[...]

    def front(i, c, parts=False):
        @pl.when(s == 0)
        def _():
            @pl.when(i > 0)
            def _():
                l_copy(i, c).wait_recv()
            first = jnp.dot(latin[i, rows(c), :], cin[...].astype(BF16), preferred_element_type=F32).astype(BF16)
            xbuf[i, 0, rows(c), :] = first
            xbuf[i, 1, rows(c), :] = first

        @pl.when(s > 0)
        def _():
            if parts:
                if c == 0:
                    for j in range(final_piece):
                        x_part(j).wait_recv()
                x_part(final_piece, c).wait_recv()
            else:
                x_copy(ybuf.at[i, :, rows(c), :], i, c).wait_recv()

        if parts:
            if c == 0:
                for j in range(final_piece):
                    k_part(j).wait_recv()
            k_part(final_piece, c).wait_recv()
        else:
            k_copy(ybuf.at[i, :, rows(c), :], i, c).wait_recv()
        time_vec = tv[pl.ds(i, 1), :]
        for g in range(2):
            a = 0.5 * (xbuf[i, g, rows(c), :].astype(F32) + kbuf[i, g, rows(c), :].astype(F32)) + time_vec
            if g == 0:
                a = a + cond[...]
            a_scr[c, g * part:(g + 1) * part, :] = a
        a = a_scr[c]
        normed = (a * lax.rsqrt(jnp.mean(a * a, axis=-1, keepdims=True) + 1e-6)).astype(BF16)
        tile = 256 if hidden % 256 == 0 else hidden
        for j in range(0, hidden, tile):
            gate = jnp.dot(normed, w_in[:, hidden + j:hidden + j + tile], preferred_element_type=F32)
            value = jnp.dot(normed, w_in[:, j:j + tile], preferred_element_type=F32)
            gelu = 0.5 * gate * (1.0 + lax.erf(gate * math.sqrt(0.5)))
            h_scr[c, :, j:j + tile] = (value * gelu).astype(BF16)

    def back(i, c):
        out = (a_scr[c] + jnp.dot(h_scr[c], w_all[...], preferred_element_type=F32)).astype(BF16)

        @pl.when(i < steps - 1)
        def _():
            ybuf[i + 1, :, rows(c), :] = out.reshape(2, part, channels)

            @pl.when((s < last) & jnp.logical_not((s == 1) & (i == held)))
            def _():
                x_copy(ybuf.at[i + 1, :, rows(c), :], i + 1, c).start()
            k_copy(ybuf.at[i + 1, :, rows(c), :], i + 1, c).start()

        @pl.when(i == steps - 1)
        def _():
            oseg_ref[:, rows(c), :] = out.reshape(2, part, channels)
        denoise(i, c, out)

    def back_piece(j, c):
        at, width = pieces[j]
        out = a_scr[c, :, at:at + width] + jnp.dot(h_scr[c], w_all[:, at:at + width], preferred_element_type=F32)
        ybuf[1, :, rows(c), at:at + width] = out.astype(BF16).reshape(2, part, width)

    def send_piece(j, c=None):
        @pl.when(s < last)
        def _():
            x_part(j, c).start()
        k_part(j, c).start()

    def denoise(i, c, out):
        @pl.when(s == last)
        def _():
            v = out.astype(F32)
            v = v * lax.rsqrt(jnp.mean(v * v, axis=-1, keepdims=True) + 1e-6)
            m = (v * (1.0 / (1.0 + jnp.exp(-v)))).astype(BF16)
            e = lax.dot_general(m, cout[...].astype(BF16), (((1,), (1,)), ((), ())), preferred_element_type=F32)
            guided = e[part:] + guidance_scale * (e[:part] - e[part:])
            root_now, root_next = roots[pl.ds(i, 1), :], roots[pl.ds(i + 1, 1), :]
            rest_now, rest_next = rests[pl.ds(i, 1), :], rests[pl.ds(i + 1, 1), :]
            clean = (lat[rows(c), :] - rest_now * guided) / root_now
            new = root_next * clean + rest_next * guided
            lat[rows(c), :] = new

            @pl.when(i < steps - 1)
            def _():
                latout[i + 1, rows(c), :] = new.astype(BF16)
                l_copy(i + 1, c).start()

    def back_pieces(j):
        for c in range(CHUNKS):
            back_piece(j, c)
            if j == final_piece:
                send_piece(j, c)
                denoise(0, c, ybuf[1, :, rows(c), :].reshape(2 * part, channels))
        if j < final_piece:
            send_piece(j)

    def fronts(c):
        if c == 0:
            loads[1].wait()
        front(0, c)

    if gathered:
        for c in range(CHUNKS):
            fronts(c)
        loads[2].wait()
        for j in range(len(pieces)):
            back_pieces(j)
    else:
        def go():
            @pl.when(even)
            def _():
                pl.semaphore_signal(turn, inc=1, device_id={"sect": s + 1}, device_id_type=MESH)

            @pl.when(jnp.logical_not(even))
            def _():
                pl.semaphore_wait(turn, 1)
                own_all()

        def stage(t):
            for k in (1, 2, 3):
                for d in (1, -1):
                    j = t - (k - 1) * LAG - (OFFSET if d < 0 else 0)
                    if 0 <= j < count:
                        passed(j, k, start, True, (d,))
            j = t - BLAG
            if j in DETOUR and j < count:
                beside(j, start, True)

        for t in range(LEAD):
            @pl.when(even)
            def _(t=t):
                stage(t)
        go()
        for t in range(LEAD):
            @pl.when(jnp.logical_not(even))
            def _(t=t):
                stage(t)

        @pl.when(z + 1 < length)
        def _():
            pl.semaphore_wait(ready.at[1], 2 * (length - 1 - z))
        p_up(start)
        for t in range(LEAD, FRONTS[0]):
            stage(t)
        for d in range(1, batches):
            b = lax.rem(me + d, batches)
            pltpu.make_async_copy(ptab.at[b], ptab.at[b], p_recv.at[b]).wait()
        cond[...] = ptab[assign_ref[0]]
        fronts(0)
        for t in range(FRONTS[0], FRONTS[1]):
            stage(t)
        for c in range(1, CHUNKS):
            fronts(c)
        for t in range(FRONTS[1], max(2 * LAG, BLAG) + count + OFFSET):
            stage(t)
        loads[2].wait()
        for j in range(count):
            piece_here(j)
            back_pieces(j)
    for c in range(CHUNKS):
        front(1, c, True)
        back(1, c)

    def body(i, carry):
        for c in range(CHUNKS):
            front(i, c)
            back(i, c)
        if held < steps:
            @pl.when((i == held) & (s == 0))
            def _():
                for c in range(CHUNKS):
                    k_copy(ybuf.at[i + 1, :, rows(c), :], i + 1, c).wait_send()
                pl.semaphore_signal(passage, inc=1, device_id={"sect": 1}, device_id_type=MESH)

            @pl.when((i == held) & (s == 1))
            def _():
                pl.semaphore_wait(passage, 1)
                for c in range(CHUNKS):
                    x_copy(ybuf.at[i + 1, :, rows(c), :], i + 1, c).start()
        return carry

    lax.fori_loop(2, steps, body, 0)

    @pl.when(s == last)
    def _():
        turned = lat[...].T
        here = olat_ref.shape[0]
        for d in range(sects):
            fin[d] = turned[d * here:(d + 1) * here, :]
        for d in range(sects - 1):
            f_copy(d).start()
        olat_ref[...] = fin[last]
        for d in range(sects - 1):
            f_copy(d).wait_send()
        for i in range(1, steps):
            for c in range(CHUNKS):
                l_copy(i, c).wait_send()

    @pl.when(s < last)
    def _():
        f_copy(0).wait_recv()
        olat_ref[...] = fin_in[...]
        for c in range(CHUNKS):
            for i in range(steps):
                if i == 1:
                    x_part(final_piece, c).wait_send()
                else:
                    x_copy(ybuf.at[i, :, rows(c), :], i, c).wait_send()
        for j in range(final_piece):
            x_part(j).wait_send()

    for c in range(CHUNKS):
        for i in range(steps):
            if i == 1:
                k_part(final_piece, c).wait_send()
            elif i == held + 1:
                @pl.when(s > 0)
                def _(i=i, c=c):
                    k_copy(ybuf.at[i, :, rows(c), :], i, c).wait_send()
            else:
                k_copy(ybuf.at[i, :, rows(c), :], i, c).wait_send()
    for j in range(final_piece):
        k_part(j).wait_send()
    if not gathered:
        p_down(sent)
        p_up(sent)
        for j in range(count):
            own_side(j, sent)
            for d in (1, -1):
                own_line(j, d, sent)
            for k in (1, 2, 3):
                passed(j, k, sent, False)
            beside(j, sent, False)


def hand_over(segment_ref, final_ref, oseg_ref, olat_ref):
    oseg_ref[...] = segment_ref[...]
    olat_ref[...] = final_ref[...]


def on_device(
    sects, batches, warm, latents, timesteps, assign, prompts, w_in, time_w, w_out, conv_in_w, conv_out_w
):
    positions = latents.shape[1]
    channels = warm.shape[1]
    hidden = w_out.shape[0] * batches
    steps = timesteps.shape[0] - 1
    gathered = w_out.shape[0] % 16 != 0 or batches != 8 or sects != 4
    if gathered:
        w_out = lax.all_gather(w_out, "batch", axis=0, tiled=True)
        table = lax.all_gather(prompts, "batch", axis=0, tiled=True)
        prompts = lax.dynamic_slice_in_dim(table, assign[0], 1, 0).astype(F32)
    whole = pl.BlockSpec(memory_space=pltpu.VMEM)
    apart = pl.BlockSpec(memory_space=pltpu.HBM)
    here = latents.shape[0] // sects
    pieces = len(column_pieces(channels))
    dma = pltpu.SemaphoreType.DMA
    slots = 1 if gathered else batches
    width = 2 * positions // CHUNKS
    segment, final = pl.pallas_call(
        functools.partial(kernel, sects, batches, gathered),
        out_shape=(
            pltpu.VMEM((2, positions, channels), BF16),
            pltpu.VMEM((here, positions), F32),
        ),
        in_specs=[apart] * 10,
        out_specs=(whole, whole),
        scratch_shapes=[
            pltpu.SMEM(timesteps.shape, jnp.int32),
            pltpu.SMEM(assign.shape, jnp.int32),
            pltpu.VMEM(latents.shape, F32),
            pltpu.VMEM(prompts.shape, prompts.dtype),
            pltpu.VMEM(conv_in_w.shape, BF16),
            pltpu.VMEM(conv_out_w.shape, BF16),
            pltpu.VMEM(w_in.shape, BF16),
            pltpu.VMEM(time_w.shape, BF16),
            pltpu.VMEM((hidden, channels), BF16),
            pltpu.VMEM((steps, 2, positions, channels), BF16),
            pltpu.VMEM((steps, 2, positions, channels), BF16),
            pltpu.VMEM((steps, 2, positions, channels), BF16),
            pltpu.VMEM((CHUNKS, width, channels), F32),
            pltpu.VMEM((CHUNKS, width, hidden), BF16),
            pltpu.VMEM((16, channels), F32),
            pltpu.VMEM((16, 128), F32),
            pltpu.VMEM((16, 128), F32),
            pltpu.VMEM((1, channels), F32),
            pltpu.VMEM((batches, 1, channels), F32),
            pltpu.VMEM((128, channels), F32),
            pltpu.VMEM((128, channels), F32),
            pltpu.VMEM((128, positions), F32),
            pltpu.VMEM((steps, positions, 128), BF16),
            pltpu.VMEM((steps, positions, 128), BF16),
            pltpu.VMEM((sects, here, positions), F32),
            pltpu.VMEM((here, positions), F32),
            pltpu.SemaphoreType.REGULAR((2,)), pltpu.SemaphoreType.REGULAR, pltpu.SemaphoreType.REGULAR,
            dma((9,)),
            dma((steps, CHUNKS)), dma((steps, CHUNKS)),
            dma((steps, CHUNKS)), dma((steps, CHUNKS)),
            dma((steps, CHUNKS)), dma((steps, CHUNKS)),
            dma((sects,)), dma(()),
            dma((slots,)), dma((slots,)),
            dma((2, pieces, slots)), dma((pieces, slots)), dma((pieces, slots)),
            dma((pieces,)), dma((pieces,)), dma((pieces,)), dma((pieces,)),
        ],
        compiler_params=pltpu.CompilerParams(
            collective_id=0, has_side_effects=True, vmem_limit_bytes=58000 * 1024
        ),
    )(
        timesteps, assign, warm.reshape(2, positions, channels), latents, prompts,
        w_in, time_w, w_out, conv_in_w, conv_out_w,
    )
    return pl.pallas_call(
        hand_over,
        out_shape=(
            jax.ShapeDtypeStruct((2 * positions, channels), BF16),
            jax.ShapeDtypeStruct((here, positions), F32),
        ),
        in_specs=[whole, whole],
        out_specs=(whole, whole),
        compiler_params=pltpu.CompilerParams(vmem_limit_bytes=4 * 1024 * 1024),
    )(segment.reshape(2 * positions, channels), final)


def solution(mesh):
    return jax.shard_map(
        functools.partial(on_device, mesh.shape["sect"], mesh.shape["batch"]),
        mesh=mesh,
        in_specs=(
            P(("sect", "batch"), None),
            P(None, "batch"),
            P(),
            P("batch"),
            P("batch", None),
            P("sect", None),
            P("sect", None),
            P(("sect", "batch"), None),
            P(),
            P(),
        ),
        out_specs=(P(("sect", "batch"), None), P("sect", "batch")),
        check_vma=False,
    )
```

```python
import functools
import math

import jax
import jax.numpy as jnp
from jax import lax
from jax.experimental import pallas as pl
from jax.experimental.pallas import tpu as pltpu
from jax.sharding import PartitionSpec as P

guidance_scale = 3.0
MESH = pl.DeviceIdType.MESH
F32 = jnp.float32
BF16 = jnp.bfloat16
CHUNKS = 2
SPLIT = (128, 128, 128, 128, 128)
DETOUR = (3, 4)
LEAD = 4
LAG = 5
BLAG = 10
OFFSET = 1
FRONTS = (9, 12)


def column_pieces(channels):
    widths = SPLIT if sum(SPLIT) == channels else (channels,)
    return [(sum(widths[:j]), width) for j, width in enumerate(widths)]


def kernel(
    sects, batches, gathered,
    ts_hbm, assign_hbm, warm_ref, lat_hbm, prompts_hbm, w_in_ref, time_w_ref, w_out_ref, cin_hbm, cout_hbm,
    oseg_ref, olat_ref,
    ts_ref, assign_ref, lat_ref, prompts_ref, cin_ref, cout_ref,
    w_in, time_w, w_all, xbuf, kbuf, ybuf, a_scr, h_scr, tv, roots, rests, cond, ptab,
    cin, cout, lat, latin, latout, fin, fin_in,
    ready, turn, passage, half_send, load_sem, x_send, x_recv, k_send, k_recv, l_send, l_recv, f_send, f_recv,
    p_send, p_recv, g_line, g_side, g_recv, xc_send, xc_recv, kc_send, kc_recv,
):
    s = lax.axis_index("sect")
    me = lax.axis_index("batch")
    steps = ts_ref.shape[0] - 1
    _, positions, channels = warm_ref.shape
    hidden = w_all.shape[0]
    part = positions // CHUNKS
    up = lax.rem(s + 1, sects)
    down = lax.rem(s + sects - 1, sects)
    last = sects - 1
    pieces = column_pieces(channels)
    final_piece = len(pieces) - 1
    held = steps - 2 if steps >= 4 and sects == 4 else steps

    loads = [
        pltpu.make_async_copy(time_w_ref, time_w, load_sem.at[0]),
        pltpu.make_async_copy(w_in_ref, w_in, load_sem.at[1]),
    ]
    if gathered:
        loads.append(pltpu.make_async_copy(w_out_ref, w_all, load_sem.at[2]))
    else:
        depth = w_out_ref.shape[0]
        own_rows = pl.ds(pl.multiple_of(me * depth, depth), depth)
        loads.append(pltpu.make_async_copy(w_out_ref, w_all.at[own_rows], load_sem.at[2]))
    pairs = [(prompts_hbm, prompts_ref), (ts_hbm, ts_ref), (assign_hbm, assign_ref), (lat_hbm, lat_ref),
             (cin_hbm, cin_ref), (cout_hbm, cout_ref)]
    for j, (src, dst) in enumerate(pairs):
        loads.append(pltpu.make_async_copy(src, dst, load_sem.at[3 + j]))
    for copy in loads[3:] + loads[:3]:
        copy.start()

    barrier = pltpu.get_barrier_semaphore()
    for d in range(1, sects):
        pl.semaphore_signal(barrier, inc=1, device_id={"sect": lax.rem(s + d, sects)}, device_id_type=MESH)
    met = sects - 1
    if not gathered:
        z, y = me // 2, lax.rem(me, 2)
        length = batches // 2
        side = z * 2 + (1 - y)
        pl.semaphore_signal(barrier, inc=1, device_id={"batch": side}, device_id_type=MESH)
        for d in range(1, length):
            @pl.when(z + d < length)
            def _(d=d):
                for b in (me + 2 * d, side + 2 * d):
                    pl.semaphore_signal(barrier, inc=1, device_id={"batch": b}, device_id_type=MESH)
        met = met + 1 + 2 * z
        loads[3].wait()
        ptab[me] = prompts_ref[...].astype(F32)
    pl.semaphore_wait(barrier, met)
    if not gathered:
        for d in range(1, length):
            @pl.when(z >= d)
            def _(d=d):
                for b in (me - 2 * d, side - 2 * d):
                    pl.semaphore_signal(ready.at[1], inc=1, device_id={"batch": b}, device_id_type=MESH)
                if d == 1:
                    pl.semaphore_signal(ready.at[0], inc=1, device_id={"batch": me - 2 * d}, device_id_type=MESH)

    def rows(c):
        return pl.ds(c * part, part)

    def x_copy(src, slot, c):
        return pltpu.make_async_remote_copy(
            src_ref=src, dst_ref=xbuf.at[slot, :, rows(c), :], send_sem=x_send.at[slot, c],
            recv_sem=x_recv.at[slot, c], device_id={"sect": up}, device_id_type=MESH)

    def k_copy(src, slot, c):
        return pltpu.make_async_remote_copy(
            src_ref=src, dst_ref=kbuf.at[slot, :, rows(c), :], send_sem=k_send.at[slot, c],
            recv_sem=k_recv.at[slot, c], device_id={"sect": down}, device_id_type=MESH)

    def k_half(slot, c, g):
        return pltpu.make_async_remote_copy(
            src_ref=ybuf.at[slot, g, rows(c), :], dst_ref=kbuf.at[slot, g, rows(c), :], send_sem=half_send.at[g],
            recv_sem=k_recv.at[slot, c], device_id={"sect": down}, device_id_type=MESH)

    def columns(ref, j, c=None):
        at, width = pieces[j]
        return ref.at[1, :, slice(None) if c is None else rows(c), pl.ds(at, width)]

    def x_part(j, c=None):
        sems = (xc_send.at[j], xc_recv.at[j]) if c is None else (x_send.at[1, c], x_recv.at[1, c])
        return pltpu.make_async_remote_copy(
            src_ref=columns(ybuf, j, c), dst_ref=columns(xbuf, j, c), send_sem=sems[0],
            recv_sem=sems[1], device_id={"sect": up}, device_id_type=MESH)

    def k_part(j, c=None):
        sems = (kc_send.at[j], kc_recv.at[j]) if c is None else (k_send.at[1, c], k_recv.at[1, c])
        return pltpu.make_async_remote_copy(
            src_ref=columns(ybuf, j, c), dst_ref=columns(kbuf, j, c), send_sem=sems[0],
            recv_sem=sems[1], device_id={"sect": down}, device_id_type=MESH)

    def l_copy(slot, c):
        return pltpu.make_async_remote_copy(
            src_ref=latout.at[slot, rows(c), :], dst_ref=latin.at[slot, rows(c), :], send_sem=l_send.at[slot, c],
            recv_sem=l_recv.at[slot, c], device_id={"sect": 0}, device_id_type=MESH)

    def f_copy(d):
        return pltpu.make_async_remote_copy(
            src_ref=fin.at[d], dst_ref=fin_in, send_sem=f_send.at[d],
            recv_sem=f_recv, device_id={"sect": d}, device_id_type=MESH)

    if not gathered:
        def p_copy(b):
            return pltpu.make_async_remote_copy(
                src_ref=ptab.at[me], dst_ref=ptab.at[me], send_sem=p_send.at[b], recv_sem=p_recv.at[me],
                device_id={"batch": b}, device_id_type=MESH)

        def p_down(act):
            act(p_copy(side))
            for d in range(1, length):
                @pl.when(z >= d)
                def _(d=d):
                    act(p_copy(me - 2 * d))
                    act(p_copy(side - 2 * d))

        def p_up(act):
            for d in range(1, length):
                @pl.when(z + d < length)
                def _(d=d):
                    act(p_copy(me + 2 * d))
                    act(p_copy(side + 2 * d))

        def block(j, b):
            at, width = pieces[j]
            return w_all.at[pl.ds(pl.multiple_of(b * depth, depth), depth), pl.ds(at, width)]

        def g_copy(j, b, to, sem, own):
            at, width = pieces[j]
            return pltpu.make_async_remote_copy(
                src_ref=w_out_ref.at[:, pl.ds(at, width)] if own else block(j, b), dst_ref=block(j, b), send_sem=sem,
                recv_sem=g_recv.at[j, b], device_id={"batch": to}, device_id_type=MESH)

        def g_line_copy(j, b, d, own=False):
            return g_copy(j, b, me + 2 * d, g_line.at[0 if d > 0 else 1, j, b], own)

        def g_side_copy(j, b, own=False):
            return g_copy(j, b, side, g_side.at[j, b], own)

        def g_arrived(j, b):
            pltpu.make_async_copy(block(j, b), block(j, b), g_recv.at[j, b]).wait()

        def own_side(j, act):
            act(g_side_copy(j, me, True))

        def own_line(j, d, act):
            @pl.when((z + d < length) & (z + d >= 0))
            def _():
                act(g_line_copy(j, me, d, True))

        def passed(j, k, act, arrive, dirs=(1, -1)):
            detour = j in DETOUR and k == 1
            for d in dirs:
                @pl.when((z + d * k < length) & (z + d * k >= 0))
                def _(d=d):
                    b = me + 2 * d * k
                    if arrive:
                        g_arrived(j, b)

                    @pl.when((z - d < length) & (z - d >= 0))
                    def _():
                        act(g_line_copy(j, b, -d))
                    if not detour:
                        act(g_side_copy(j, b))
                    elif d > 0:
                        @pl.when(z > 0)
                        def _():
                            act(g_side_copy(j, b))

        def beside(j, act, arrive):
            if arrive:
                g_arrived(j, side)
            if j in DETOUR:
                @pl.when(z + 1 < length)
                def _():
                    act(g_line_copy(j, side, 1))

                @pl.when(z == 1)
                def _():
                    act(g_line_copy(j, side, -1))

        def start(copy):
            copy.start()

        def sent(copy):
            copy.wait_send()

        def piece_here(j):
            for k in range(length):
                b = 2 * k + (1 - y)

                if j not in DETOUR:
                    g_arrived(j, b)
                else:
                    @pl.when(b != side)
                    def _():
                        g_arrived(j, b)

        count = len(pieces)

        def own_all():
            for j in range(count):
                own_line(j, -1, start)
                own_side(j, start)

            @pl.when(z + 1 < length)
            def _():
                pl.semaphore_wait(ready.at[0], 1)
            for j in range(count):
                own_line(j, 1, start)

        even = lax.rem(s, 2) == 0
        p_down(start)

        @pl.when(even)
        def _():
            own_all()

    for c in range(CHUNKS):
        @pl.when(s < last)
        def _(c=c):
            x_copy(warm_ref.at[:, rows(c), :], 0, c).start()
        k_copy(warm_ref.at[:, rows(c), :], 0, c).start()

    if gathered:
        loads[3].wait()
    for copy in loads[4:]:
        copy.wait()
    cin[...] = jnp.zeros_like(cin)
    cout[...] = jnp.zeros_like(cout)
    levels = cin_ref.shape[0]
    cin[0:levels, :] = cin_ref[...].astype(F32)
    cout[0:levels, :] = cout_ref[...].astype(F32)
    lat[...] = jnp.zeros_like(lat)
    lat[0:levels, :] = lat_ref[...]
    turned = lat[...].T
    lat[...] = turned
    latin[0] = turned.astype(BF16)
    which = lax.broadcasted_iota(jnp.int32, (16, 128), 0)
    times = jnp.zeros((16, 128), F32)
    for i in range(steps + 1):
        times = jnp.where(which == i, ts_ref[i].astype(F32), times)
    bar = jnp.cos((times / 1000.0 + 0.008) / 1.008 * (math.pi / 2)) ** 2
    roots[...] = jnp.sqrt(bar)
    rests[...] = jnp.sqrt(1.0 - bar)
    half = channels // 2
    lane = lax.broadcasted_iota(jnp.int32, (16, channels), 1)
    wave = jnp.where(lane < half, lane, lane - half).astype(F32)
    frequency = jnp.exp(-math.log(10000.0) * wave / half)
    angles = jnp.concatenate([times] * (channels // 128), axis=1) * frequency
    waves = jnp.where(lane < half, jnp.cos(angles), jnp.sin(angles))
    embedded = (waves * (1.0 / (1.0 + jnp.exp(-waves)))).astype(BF16)
    loads[0].wait()
    tv[...] = jnp.dot(embedded, time_w[...], preferred_element_type=F32)

    if gathered:
        cond[...] = prompts_ref[...]

    def front(i, c, parts=False):
        @pl.when(s == 0)
        def _():
            @pl.when(i > 0)
            def _():
                l_copy(i, c).wait_recv()
            first = jnp.dot(latin[i, rows(c), :], cin[...].astype(BF16), preferred_element_type=F32).astype(BF16)
            xbuf[i, 0, rows(c), :] = first
            xbuf[i, 1, rows(c), :] = first

        @pl.when(s > 0)
        def _():
            if parts:
                if c == 0:
                    for j in range(final_piece):
                        x_part(j).wait_recv()
                x_part(final_piece, c).wait_recv()
            else:
                x_copy(ybuf.at[i, :, rows(c), :], i, c).wait_recv()

        if parts:
            if c == 0:
                for j in range(final_piece):
                    k_part(j).wait_recv()
            k_part(final_piece, c).wait_recv()
        else:
            k_copy(ybuf.at[i, :, rows(c), :], i, c).wait_recv()
        time_vec = tv[pl.ds(i, 1), :]
        for g in range(2):
            a = 0.5 * (xbuf[i, g, rows(c), :].astype(F32) + kbuf[i, g, rows(c), :].astype(F32)) + time_vec
            if g == 0:
                a = a + cond[...]
            a_scr[c, g * part:(g + 1) * part, :] = a
        a = a_scr[c]
        normed = (a * lax.rsqrt(jnp.mean(a * a, axis=-1, keepdims=True) + 1e-6)).astype(BF16)
        tile = 256 if hidden % 256 == 0 else hidden
        for j in range(0, hidden, tile):
            gate = jnp.dot(normed, w_in[:, hidden + j:hidden + j + tile], preferred_element_type=F32)
            value = jnp.dot(normed, w_in[:, j:j + tile], preferred_element_type=F32)
            gelu = 0.5 * gate * (1.0 + lax.erf(gate * math.sqrt(0.5)))
            h_scr[c, :, j:j + tile] = (value * gelu).astype(BF16)

    def back(i, c):
        out = (a_scr[c] + jnp.dot(h_scr[c], w_all[...], preferred_element_type=F32)).astype(BF16)

        @pl.when(i < steps - 1)
        def _():
            ybuf[i + 1, :, rows(c), :] = out.reshape(2, part, channels)

            @pl.when((s < last) & jnp.logical_not((s == 1) & (i == held)))
            def _():
                x_copy(ybuf.at[i + 1, :, rows(c), :], i + 1, c).start()
            halved = (s == 0) & (i == held) if c == CHUNKS - 1 else s < 0

            @pl.when(halved)
            def _():
                k_half(i + 1, c, 0).start()
                k_half(i + 1, c, 1).start()

            @pl.when(jnp.logical_not(halved))
            def _():
                k_copy(ybuf.at[i + 1, :, rows(c), :], i + 1, c).start()

        @pl.when(i == steps - 1)
        def _():
            oseg_ref[:, rows(c), :] = out.reshape(2, part, channels)
        denoise(i, c, out)

    def back_piece(j, c):
        at, width = pieces[j]
        out = a_scr[c, :, at:at + width] + jnp.dot(h_scr[c], w_all[:, at:at + width], preferred_element_type=F32)
        ybuf[1, :, rows(c), at:at + width] = out.astype(BF16).reshape(2, part, width)

    def send_piece(j, c=None):
        @pl.when(s < last)
        def _():
            x_part(j, c).start()
        k_part(j, c).start()

    def denoise(i, c, out):
        @pl.when(s == last)
        def _():
            v = out.astype(F32)
            v = v * lax.rsqrt(jnp.mean(v * v, axis=-1, keepdims=True) + 1e-6)
            m = (v * (1.0 / (1.0 + jnp.exp(-v)))).astype(BF16)
            e = lax.dot_general(m, cout[...].astype(BF16), (((1,), (1,)), ((), ())), preferred_element_type=F32)
            guided = e[part:] + guidance_scale * (e[:part] - e[part:])
            root_now, root_next = roots[pl.ds(i, 1), :], roots[pl.ds(i + 1, 1), :]
            rest_now, rest_next = rests[pl.ds(i, 1), :], rests[pl.ds(i + 1, 1), :]
            clean = (lat[rows(c), :] - rest_now * guided) / root_now
            new = root_next * clean + rest_next * guided
            lat[rows(c), :] = new

            @pl.when(i < steps - 1)
            def _():
                latout[i + 1, rows(c), :] = new.astype(BF16)
                l_copy(i + 1, c).start()

    def back_pieces(j):
        for c in range(CHUNKS):
            back_piece(j, c)
            if j == final_piece:
                send_piece(j, c)
                denoise(0, c, ybuf[1, :, rows(c), :].reshape(2 * part, channels))
        if j < final_piece:
            send_piece(j)

    def fronts(c):
        if c == 0:
            loads[1].wait()
        front(0, c)

    if gathered:
        for c in range(CHUNKS):
            fronts(c)
        loads[2].wait()
        for j in range(len(pieces)):
            back_pieces(j)
    else:
        def go():
            @pl.when(even)
            def _():
                pl.semaphore_signal(turn, inc=1, device_id={"sect": s + 1}, device_id_type=MESH)

            @pl.when(jnp.logical_not(even))
            def _():
                pl.semaphore_wait(turn, 1)
                own_all()

        def stage(t):
            for k in (1, 2, 3):
                for d in (1, -1):
                    j = t - (k - 1) * LAG - (OFFSET if d < 0 else 0)
                    if 0 <= j < count:
                        passed(j, k, start, True, (d,))
            j = t - BLAG
            if j in DETOUR and j < count:
                beside(j, start, True)

        for t in range(LEAD):
            @pl.when(even)
            def _(t=t):
                stage(t)
        go()
        for t in range(LEAD):
            @pl.when(jnp.logical_not(even))
            def _(t=t):
                stage(t)

        @pl.when(z + 1 < length)
        def _():
            pl.semaphore_wait(ready.at[1], 2 * (length - 1 - z))
        p_up(start)
        for t in range(LEAD, FRONTS[0]):
            stage(t)
        for d in range(1, batches):
            b = lax.rem(me + d, batches)
            pltpu.make_async_copy(ptab.at[b], ptab.at[b], p_recv.at[b]).wait()
        cond[...] = ptab[assign_ref[0]]
        fronts(0)
        for t in range(FRONTS[0], FRONTS[1]):
            stage(t)
        for c in range(1, CHUNKS):
            fronts(c)
        for t in range(FRONTS[1], max(2 * LAG, BLAG) + count + OFFSET):
            stage(t)
        loads[2].wait()
        for j in range(count):
            piece_here(j)
            back_pieces(j)
    for c in range(CHUNKS):
        front(1, c, True)
        back(1, c)

    def body(i, carry):
        for c in range(CHUNKS):
            front(i, c)
            back(i, c)
        if held < steps:
            @pl.when((i == held) & (s == 0))
            def _():
                for c in range(CHUNKS - 1):
                    k_copy(ybuf.at[i + 1, :, rows(c), :], i + 1, c).wait_send()
                k_half(i + 1, CHUNKS - 1, 0).wait_send()
                pl.semaphore_signal(passage, inc=1, device_id={"sect": 1}, device_id_type=MESH)
                k_half(i + 1, CHUNKS - 1, 1).wait_send()

            @pl.when((i == held) & (s == 1))
            def _():
                pl.semaphore_wait(passage, 1)
                for c in range(CHUNKS):
                    x_copy(ybuf.at[i + 1, :, rows(c), :], i + 1, c).start()
        return carry

    lax.fori_loop(2, steps, body, 0)

    @pl.when(s == last)
    def _():
        turned = lat[...].T
        here = olat_ref.shape[0]
        for d in range(sects):
            fin[d] = turned[d * here:(d + 1) * here, :]
        for d in range(sects - 1):
            f_copy(d).start()
        olat_ref[...] = fin[last]
        for d in range(sects - 1):
            f_copy(d).wait_send()
        for i in range(1, steps):
            for c in range(CHUNKS):
                l_copy(i, c).wait_send()

    @pl.when(s < last)
    def _():
        f_copy(0).wait_recv()
        olat_ref[...] = fin_in[...]
        for c in range(CHUNKS):
            for i in range(steps):
                if i == 1:
                    x_part(final_piece, c).wait_send()
                else:
                    x_copy(ybuf.at[i, :, rows(c), :], i, c).wait_send()
        for j in range(final_piece):
            x_part(j).wait_send()

    for c in range(CHUNKS):
        for i in range(steps):
            if i == 1:
                k_part(final_piece, c).wait_send()
            elif i == held + 1:
                @pl.when(s > 0)
                def _(i=i, c=c):
                    k_copy(ybuf.at[i, :, rows(c), :], i, c).wait_send()
            else:
                k_copy(ybuf.at[i, :, rows(c), :], i, c).wait_send()
    for j in range(final_piece):
        k_part(j).wait_send()
    if not gathered:
        p_down(sent)
        p_up(sent)
        for j in range(count):
            own_side(j, sent)
            for d in (1, -1):
                own_line(j, d, sent)
            for k in (1, 2, 3):
                passed(j, k, sent, False)
            beside(j, sent, False)


def hand_over(segment_ref, final_ref, oseg_ref, olat_ref):
    oseg_ref[...] = segment_ref[...]
    olat_ref[...] = final_ref[...]


def on_device(
    sects, batches, warm, latents, timesteps, assign, prompts, w_in, time_w, w_out, conv_in_w, conv_out_w
):
    positions = latents.shape[1]
    channels = warm.shape[1]
    hidden = w_out.shape[0] * batches
    steps = timesteps.shape[0] - 1
    gathered = w_out.shape[0] % 16 != 0 or batches != 8 or sects != 4
    if gathered:
        w_out = lax.all_gather(w_out, "batch", axis=0, tiled=True)
        table = lax.all_gather(prompts, "batch", axis=0, tiled=True)
        prompts = lax.dynamic_slice_in_dim(table, assign[0], 1, 0).astype(F32)
    whole = pl.BlockSpec(memory_space=pltpu.VMEM)
    apart = pl.BlockSpec(memory_space=pltpu.HBM)
    here = latents.shape[0] // sects
    pieces = len(column_pieces(channels))
    dma = pltpu.SemaphoreType.DMA
    slots = 1 if gathered else batches
    width = 2 * positions // CHUNKS
    segment, final = pl.pallas_call(
        functools.partial(kernel, sects, batches, gathered),
        out_shape=(
            pltpu.VMEM((2, positions, channels), BF16),
            pltpu.VMEM((here, positions), F32),
        ),
        in_specs=[apart] * 10,
        out_specs=(whole, whole),
        scratch_shapes=[
            pltpu.SMEM(timesteps.shape, jnp.int32),
            pltpu.SMEM(assign.shape, jnp.int32),
            pltpu.VMEM(latents.shape, F32),
            pltpu.VMEM(prompts.shape, prompts.dtype),
            pltpu.VMEM(conv_in_w.shape, BF16),
            pltpu.VMEM(conv_out_w.shape, BF16),
            pltpu.VMEM(w_in.shape, BF16),
            pltpu.VMEM(time_w.shape, BF16),
            pltpu.VMEM((hidden, channels), BF16),
            pltpu.VMEM((steps, 2, positions, channels), BF16),
            pltpu.VMEM((steps, 2, positions, channels), BF16),
            pltpu.VMEM((steps, 2, positions, channels), BF16),
            pltpu.VMEM((CHUNKS, width, channels), F32),
            pltpu.VMEM((CHUNKS, width, hidden), BF16),
            pltpu.VMEM((16, channels), F32),
            pltpu.VMEM((16, 128), F32),
            pltpu.VMEM((16, 128), F32),
            pltpu.VMEM((1, channels), F32),
            pltpu.VMEM((batches, 1, channels), F32),
            pltpu.VMEM((128, channels), F32),
            pltpu.VMEM((128, channels), F32),
            pltpu.VMEM((128, positions), F32),
            pltpu.VMEM((steps, positions, 128), BF16),
            pltpu.VMEM((steps, positions, 128), BF16),
            pltpu.VMEM((sects, here, positions), F32),
            pltpu.VMEM((here, positions), F32),
            pltpu.SemaphoreType.REGULAR((2,)), pltpu.SemaphoreType.REGULAR, pltpu.SemaphoreType.REGULAR,
            dma((2,)),
            dma((9,)),
            dma((steps, CHUNKS)), dma((steps, CHUNKS)),
            dma((steps, CHUNKS)), dma((steps, CHUNKS)),
            dma((steps, CHUNKS)), dma((steps, CHUNKS)),
            dma((sects,)), dma(()),
            dma((slots,)), dma((slots,)),
            dma((2, pieces, slots)), dma((pieces, slots)), dma((pieces, slots)),
            dma((pieces,)), dma((pieces,)), dma((pieces,)), dma((pieces,)),
        ],
        compiler_params=pltpu.CompilerParams(
            collective_id=0, has_side_effects=True, vmem_limit_bytes=58000 * 1024
        ),
    )(
        timesteps, assign, warm.reshape(2, positions, channels), latents, prompts,
        w_in, time_w, w_out, conv_in_w, conv_out_w,
    )
    return pl.pallas_call(
        hand_over,
        out_shape=(
            jax.ShapeDtypeStruct((2 * positions, channels), BF16),
            jax.ShapeDtypeStruct((here, positions), F32),
        ),
        in_specs=[whole, whole],
        out_specs=(whole, whole),
        compiler_params=pltpu.CompilerParams(vmem_limit_bytes=4 * 1024 * 1024),
    )(segment.reshape(2 * positions, channels), final)


def solution(mesh):
    return jax.shard_map(
        functools.partial(on_device, mesh.shape["sect"], mesh.shape["batch"]),
        mesh=mesh,
        in_specs=(
            P(("sect", "batch"), None),
            P(None, "batch"),
            P(),
            P("batch"),
            P("batch", None),
            P("sect", None),
            P("sect", None),
            P(("sect", "batch"), None),
            P(),
            P(),
        ),
        out_specs=(P(("sect", "batch"), None), P("sect", "batch")),
        check_vma=False,
    )
```
